32 devices in a mesh: zone: 8 (over z, y), band: 4 (over x, core).
Axes of the slice: x: 2, y: 2, z: 4, core: 2. Of those that a mesh axis runs over, the one named last changes fastest.
Arguments:
- pixels: float32 [4096, 32, 128], P(('zone', 'band')), may hold values from -6 to 6
- inv_var: float32 [4096, 32, 128], P(('zone', 'band')), may hold values from 0.25 to 4
- tile_offset: float32 [2, 4096], P(None, ('zone', 'band')), may hold values from 12 to 116, as said below
- psf_amp: float32 [3, 4096], P(None, ('zone', 'band')), may hold values from 0.3 to 1
- psf_sigma: float32 [3, 4096], P(None, ('zone', 'band')), may hold values from 0.9 to 2
- tile_blob: int32 [4096], P(('zone', 'band')), may hold values from 0 to 511, as said below
- tile_band: int32 [4096], P(('zone', 'band')), may hold values from 0 to 2
- source_pos: float32 [2, 4096], P(None, 'zone'), may hold values from -5.3 to 5.3
- edge_rows: int32 [1024], P('zone'), may hold values from 0 to 511, as said below
- blob_members: int32 [512, 16], P('zone'), may hold values from 0 to 639, as said below
- sources_per_blob: int32 [512], P('zone'), may hold values from 1 to 16, as said below
Outputs:
- fluxes: float32 [3, 4096], P(None, 'zone')
The draws below stay inside these ranges and needn't reach their ends.
Inputs may be any that keep to these rules, and one draw needn't show every extreme that they name: `tile_blob`: blob b lies in zone b // 64. Of one device's 128 tiles at most 32 cover blobs of one zone, and in every draw some zone receives exactly 32 tiles from every device of each band group. `edge_rows`: per zone, 64 lower edge rows then 64 upper edge rows, local row numbers, all 128 distinct. `blob_members`: slots at or beyond the blob's count hold 0. Every source is the live member of exactly one blob: a zone's lower edge rows belong to blobs of the previous zone and its upper edge rows to blobs of the next zone, except the first zone's lower and the last zone's upper rows, which stay in their own zone; the first zone never names the first 64 entries, the last zone never the last 64. `sources_per_blob`: the counts of one zone sum to 512; in every zone some blob has 16. `tile_offset`: row offsets lie within 12 to 20.
All inputs are finite; a program needn't handle non-finite values.
Results may differ from the reference program's by a relative error of at most 0.0003.
Values sent between devices are 32-bit elements; how exact they have to be, the bound alone decides.
A program may use at most 64 MiB of HBM per device.

```python
import math
import jax
import jax.numpy as jnp
from jax import lax

FILTER_BANDS = 3
COMPS = 3
MAX_SOURCES = 16
PH = 32
PW = 128
SRC_DEV = 512
TILE_DEV = 128
BLOB_DEV = 64
EDGE = 64
CAP = 32
TILES = 4096
N_ZONE = 8
N_BAND = 4


def layout(key):
    key = jax.random.fold_in(key, 31)
    key_edge, key_claim, key_full, key_cells = jax.random.split(key, 4)
    extent = SRC_DEV + 2 * EDGE
    zone_ids = jnp.arange(N_ZONE, dtype=jnp.int32)
    edge_lists = jax.vmap(lambda sub_key: jax.random.permutation(sub_key, SRC_DEV)[:2 * EDGE])(jax.random.split(key_edge, N_ZONE)).astype(jnp.int32)
    lower_rows = edge_lists[:, :EDGE]
    upper_rows = edge_lists[:, EDGE:]

    def one_zone(zone_id, lower_list, upper_list, claim_key, full_key, cells_key):
        own_flags = jnp.ones((SRC_DEV,), jnp.int32)
        own_flags = own_flags.at[lower_list].set(jnp.where(zone_id > 0, 0, 1))
        own_flags = own_flags.at[upper_list].set(jnp.where(zone_id < N_ZONE - 1, 0, 1))
        before_flags = jnp.full((EDGE,), jnp.where(zone_id > 0, 1, 0), jnp.int32)
        after_flags = jnp.full((EDGE,), jnp.where(zone_id < N_ZONE - 1, 1, 0), jnp.int32)
        claimed = jnp.concatenate([before_flags, own_flags, after_flags])
        shuffle = jax.random.permutation(claim_key, extent).astype(jnp.int32)
        ranking = jnp.where(claimed == 1, shuffle, shuffle + extent)
        claim_order = jnp.argsort(ranking).astype(jnp.int32)
        cell_total = BLOB_DEV * (MAX_SOURCES - 1)
        full_blob = jax.random.randint(full_key, (), 0, BLOB_DEV)
        cell_shuffle = jax.random.permutation(cells_key, cell_total).astype(jnp.int32)
        cell_blob = jnp.arange(cell_total, dtype=jnp.int32) // (MAX_SOURCES - 1)
        cell_score = jnp.where(cell_blob == full_blob, cell_shuffle - cell_total, cell_shuffle)
        cell_rank = jnp.argsort(jnp.argsort(cell_score)).astype(jnp.int32)
        chosen = (cell_rank < SRC_DEV - BLOB_DEV).astype(jnp.int32)
        counts = 1 + jnp.sum(chosen.reshape(BLOB_DEV, MAX_SOURCES - 1), axis=1)
        starts = jnp.cumsum(counts) - counts
        slot_ids = jnp.arange(MAX_SOURCES, dtype=jnp.int32)
        live_slots = slot_ids[None, :] < counts[:, None]
        picks = jnp.clip(starts[:, None] + slot_ids[None, :], 0, SRC_DEV - 1)
        members = jnp.where(live_slots, claim_order[picks], 0).astype(jnp.int32)
        slot_table = jnp.broadcast_to(slot_ids[None, :], members.shape)
        slot_of = jnp.zeros((extent,), jnp.int32).at[jnp.where(live_slots, members, extent)].set(slot_table, mode='drop')
        return (members, counts.astype(jnp.int32), slot_of)
    members, counts, slot_of = jax.vmap(one_zone)(zone_ids, lower_rows, upper_rows, jax.random.split(key_claim, N_ZONE), jax.random.split(key_full, N_ZONE), jax.random.split(key_cells, N_ZONE))
    own_slots = slot_of[:, EDGE:EDGE + SRC_DEV]
    next_parts = slot_of[:, EDGE + SRC_DEV:]
    prev_parts = slot_of[:, :EDGE]
    lower_values = jnp.concatenate([next_parts[:1], next_parts[:-1]], axis=0)
    upper_values = jnp.concatenate([prev_parts[1:], prev_parts[-1:]], axis=0)

    def place(slots, lower_list, upper_list, lower_vals, upper_vals, zone_id):
        slots = slots.at[lower_list].set(jnp.where(zone_id > 0, lower_vals, slots[lower_list]))
        slots = slots.at[upper_list].set(jnp.where(zone_id < N_ZONE - 1, upper_vals, slots[upper_list]))
        return slots
    source_slots = jax.vmap(place)(own_slots, lower_rows, upper_rows, lower_values, upper_values, zone_ids)
    return (edge_lists, members, counts, source_slots)


def draw_edge_rows(key, part):
    return layout(key)[0].reshape(-1)


def draw_blob_members(key, part):
    return layout(key)[1].reshape(-1, MAX_SOURCES)


def draw_sources_per_blob(key, part):
    return layout(key)[2].reshape(-1)


def draw_source_pos(key, part):
    source_slots = layout(key)[3]
    jitter_key = jax.random.fold_in(key, 57)
    jitter_reach = 0.5
    jitter_noise = jax.random.uniform(jitter_key, (2, N_ZONE * SRC_DEV), jnp.float32, -jitter_reach, jitter_reach)
    flat_slots = source_slots.reshape(-1)
    lattice_row = (flat_slots // 4).astype(jnp.float32) * 3.0 - 4.5
    lattice_col = (flat_slots % 4).astype(jnp.float32) * 3.0 - 4.5
    return jnp.stack([lattice_row, lattice_col]) + jitter_noise


def draw_tile_offset(key, part):
    key = jax.random.fold_in(key, 97)
    row_key, col_key = jax.random.split(key)
    offset_rows = jax.random.uniform(row_key, (TILES,), jnp.float32, 12.0, 20.0)
    offset_cols = jax.random.uniform(col_key, (TILES,), jnp.float32, 12.0, PW - 12.0)
    return jnp.stack([offset_rows, offset_cols])


def draw_tile_blob(key, part):
    key = jax.random.fold_in(key, 83)
    key_busy, key_slots, key_order, key_local = jax.random.split(key, 4)
    holders = N_ZONE * N_BAND
    busy_zone = jax.random.randint(key_busy, (), 0, N_ZONE)
    free_slots = (N_ZONE - 1) * CAP
    picked = jax.vmap(lambda sub_key: jax.random.permutation(sub_key, free_slots)[:TILE_DEV - CAP])(jax.random.split(key_slots, holders))
    other_zone = (busy_zone + 1 + picked // CAP) % N_ZONE
    zone_list = jnp.concatenate([jnp.full((holders, CAP), busy_zone, jnp.int32), other_zone.astype(jnp.int32)], axis=1)
    order_perm = jax.vmap(lambda sub_key: jax.random.permutation(sub_key, TILE_DEV))(jax.random.split(key_order, holders))
    zone_list = jnp.take_along_axis(zone_list, order_perm, axis=1)
    local_blob = jax.random.randint(key_local, (holders, TILE_DEV), 0, BLOB_DEV)
    return (zone_list * BLOB_DEV + local_blob).reshape(-1).astype(jnp.int32)


def place_ends(drawn, stream_key, least, high):
    shape = drawn.shape
    spot = [jax.random.randint(jax.random.fold_in(stream_key, axis), (), 0, shape[axis]) for axis in range(len(shape))]
    drawn = drawn.at[tuple(spot)].set(least)
    longest = shape.index(max(shape))
    spot[longest] = (spot[longest] + 1) % shape[longest]
    return drawn.at[tuple(spot)].set(high)


def block_levels(key, shape, shards, smallest, largest):
    level = 1.0
    for dim, parts in shards:
        draws = jax.random.uniform(jax.random.fold_in(jax.random.fold_in(key, 6), dim), (parts,), jnp.float32, smallest / len(shards), largest / len(shards))
        level = level * jnp.repeat(jnp.exp(draws), shape[dim] // parts).reshape((-1,) + (1,) * (len(shape) - 1 - dim))
    return level


def centred(rng, shape, scale, bound, pieces=(), kind=jnp.bfloat16):
    drawn = scale * jax.random.normal(rng, shape, jnp.float32)
    if pieces:
        drawn = drawn * block_levels(rng, shape, pieces, -0.22, 0.18)
    return jnp.clip(drawn, -bound, bound).astype(kind)


def setup_inputs(seed: int = 0) -> dict:
    seeds = jax.random.split(jax.random.key(seed), 12)
    return {
        "pixels": centred(seeds[0], (TILES, PH, PW), 1.0, 6.0, ((0, 32),), jnp.float32),
        "inv_var": jnp.clip(jnp.exp(math.log(4.0) - 2.7725887 * jax.random.uniform(seeds[1], (TILES, PH, PW), jnp.float32) ** block_levels(seeds[1], (TILES, PH, PW), ((0, 32),), -0.2, 0.2)), 0.25, 4.0),
        "tile_offset": draw_tile_offset(jax.random.fold_in(seeds[11], 71), 0),
        "psf_amp": jnp.clip(jnp.exp(math.log(1.0) - 1.2039728 * jax.random.uniform(seeds[3], (COMPS, TILES), jnp.float32) ** block_levels(seeds[3], (COMPS, TILES), ((1, 32),), -0.2, 0.2)), 0.3, 1.0),
        "psf_sigma": jnp.clip(jnp.exp(math.log(2.0) - 0.798507723 * jax.random.uniform(seeds[4], (COMPS, TILES), jnp.float32) ** block_levels(seeds[4], (COMPS, TILES), ((1, 32),), -0.2, 0.2)), 0.9, 2.0),
        "tile_blob": draw_tile_blob(jax.random.fold_in(seeds[11], 71), 0),
        "tile_band": place_ends(jax.random.randint(seeds[6], (TILES,), 0, FILTER_BANDS), jax.random.fold_in(seeds[6], 1), 0, FILTER_BANDS - 1).astype(jnp.int32),
        "source_pos": draw_source_pos(jax.random.fold_in(seeds[11], 71), 0),
        "edge_rows": draw_edge_rows(jax.random.fold_in(seeds[11], 71), 0),
        "blob_members": draw_blob_members(jax.random.fold_in(seeds[11], 71), 0),
        "sources_per_blob": draw_sources_per_blob(jax.random.fold_in(seeds[11], 71), 0),
    }


HIGH = lax.Precision.HIGHEST
PRIOR = 1.0

def terms_per_tile(tile_image_pixels, tile_weight_pixels, pixel_shift, source_amplitude, profile_widths, source_location, slot_alive_flags):
    pixel_rows = jnp.arange(tile_image_pixels.shape[0]).astype(jnp.float32)
    pixel_cols = jnp.arange(tile_image_pixels.shape[1]).astype(jnp.float32)
    inverse_spread = 0.5 / (profile_widths * profile_widths)
    row_displacement = pixel_rows[None, :] - pixel_shift[0] - source_location[0][:, None]
    delta_col = pixel_cols[None, :] - pixel_shift[1] - source_location[1][:, None]
    row_profile = jnp.exp(-inverse_spread[None, :, None] * (row_displacement * row_displacement)[:, None, :]) * (source_amplitude[None, :, None] * slot_alive_flags[:, None, None])
    profile_col = jnp.exp(-inverse_spread[None, :, None] * (delta_col * delta_col)[:, None, :])
    rendered = jnp.sum(row_profile[:, :, :, None] * profile_col[:, :, None, :], axis=1).reshape(row_profile.shape[0], -1)
    weighted = rendered * tile_weight_pixels.reshape(1, -1)
    normal = jnp.einsum('sp,tp->st', weighted, rendered, precision=HIGH)
    projected = jnp.einsum('sp,p->s', weighted, tile_image_pixels.reshape(-1), precision=HIGH)
    return (normal, projected)

def reference(pixels, inv_var, tile_offset, psf_amp, psf_sigma, tile_blob, tile_band, source_pos, edge_rows, blob_members, sources_per_blob):
    blob_total = BLOB_DEV * N_ZONE
    edges = edge_rows.reshape(N_ZONE, 2, EDGE)
    zone_of = (jnp.arange(blob_total, dtype=jnp.int32) // BLOB_DEV)[:, None]
    before_zone = jnp.clip(zone_of - 1, 0, N_ZONE - 1)
    after_zone = jnp.clip(zone_of + 1, 0, N_ZONE - 1)
    from_prev = edges[before_zone, 1, jnp.clip(blob_members, 0, EDGE - 1)] + before_zone * SRC_DEV
    from_own = zone_of * SRC_DEV + jnp.clip(blob_members - EDGE, 0, SRC_DEV - 1)
    from_next = edges[after_zone, 0, jnp.clip(blob_members - EDGE - SRC_DEV, 0, EDGE - 1)] + after_zone * SRC_DEV
    source_of = jnp.where(blob_members < EDGE, from_prev, jnp.where(blob_members < EDGE + SRC_DEV, from_own, from_next)).astype(jnp.int32)
    alive = (jnp.arange(MAX_SOURCES, dtype=jnp.int32)[None, :] < sources_per_blob[:, None]).astype(jnp.float32)
    member_pos = jnp.transpose(source_pos[:, source_of], (1, 0, 2))
    tile_pos = member_pos[tile_blob]
    tile_alive = alive[tile_blob]

    def single_tile(packed):
        return terms_per_tile(*packed)
    normal, projected = lax.map(single_tile, (pixels, inv_var, tile_offset.T, psf_amp.T, psf_sigma.T, tile_pos, tile_alive), batch_size=16)
    target = (tile_blob * FILTER_BANDS + tile_band).astype(jnp.int32)
    normal_total = jax.ops.segment_sum(normal, target, num_segments=blob_total * FILTER_BANDS)
    rhs_total = jax.ops.segment_sum(projected, target, num_segments=blob_total * FILTER_BANDS)
    system = normal_total + PRIOR * jnp.eye(MAX_SOURCES, dtype=jnp.float32)[None, :, :]
    solved_fluxes = jnp.linalg.solve(system, rhs_total[:, :, None])[:, :, 0]
    value_entries = solved_fluxes.reshape(blob_total, FILTER_BANDS, MAX_SOURCES) * alive[:, None, :]
    spread = jnp.transpose(value_entries, (1, 0, 2)).reshape(FILTER_BANDS, -1)
    fluxes = jnp.zeros((FILTER_BANDS, SRC_DEV * N_ZONE), jnp.float32).at[:, source_of.reshape(-1)].add(spread)
    return fluxes
```

```python
import functools

import jax
import jax.numpy as jnp
from jax import lax
from jax.experimental import pallas as pl
from jax.experimental.pallas import tpu as pltpu
from jax.sharding import PartitionSpec as P

FILTER_BANDS = 3
COMPS = 3
MAX_SOURCES = 16
LANES = 128
PACK = LANES // MAX_SOURCES
ROWS = 24
TILES_STEP = 4
PRIOR = 1.0

VMEM = pl.BlockSpec(memory_space=pltpu.VMEM)
SMEM = pl.BlockSpec(memory_space=pltpu.SMEM)


def exchange(block, moves, pick, slot, slots, sizes, ident):
    zones, bands = sizes
    piece = block.shape[-2:] if pick is None else block.shape[1:]

    def kernel(x_ref, o_ref, send_sem, recv_sem, own_sem):
        zone = lax.axis_index("zone")
        band = lax.axis_index("band")
        targets = [
            (lax.rem(zone + dz + zones, zones), lax.rem(band + db + bands, bands))
            for dz, db in moves
        ]
        barrier = pltpu.get_barrier_semaphore()
        for target in targets:
            pl.semaphore_signal(
                barrier, inc=1, device_id=target, device_id_type=pl.DeviceIdType.MESH
            )
        own_src = x_ref if pick is None else x_ref.at[pick(zone, band)]
        own = pltpu.make_async_copy(own_src, o_ref.at[slot(0, 0, zone, band)], own_sem)
        own.start()
        pl.semaphore_wait(barrier, len(moves))
        copies = []
        for order, ((dz, db), target) in enumerate(zip(moves, targets)):
            copy = pltpu.make_async_remote_copy(
                src_ref=x_ref if pick is None else x_ref.at[pick(*target)],
                dst_ref=o_ref.at[slot(dz, db, zone, band)],
                send_sem=send_sem.at[order],
                recv_sem=recv_sem.at[order],
                device_id=target,
                device_id_type=pl.DeviceIdType.MESH,
            )
            copy.start()
            copies.append(copy)
        own.wait()
        for copy in copies:
            copy.wait()

    return pl.pallas_call(
        kernel,
        out_shape=jax.ShapeDtypeStruct((slots,) + piece, block.dtype),
        in_specs=[VMEM],
        out_specs=VMEM,
        scratch_shapes=[
            pltpu.SemaphoreType.DMA((len(moves),)),
            pltpu.SemaphoreType.DMA((len(moves),)),
            pltpu.SemaphoreType.DMA,
        ],
        compiler_params=pltpu.CompilerParams(collective_id=ident, has_side_effects=True),
    )(block)


def lane_take(row, index):
    table = jnp.broadcast_to(row, index.shape)
    return jnp.take_along_axis(table, index, axis=1, mode="promise_in_bounds")


def lookup(rows, index):
    found = jnp.zeros(index.shape, rows[0].dtype)
    low = index & (LANES - 1)
    for part, row in enumerate(rows):
        found = jnp.where(index // LANES == part, lane_take(row, low), found)
    return found


class Catalog:
    def __init__(self, sources, edge, blobs):
        self.parts = sources // LANES
        self.edge_row = 2 * self.parts
        self.count_row = self.edge_row + 1
        self.member_row = -(-(self.count_row + 1) // 8) * 8
        self.member_rows = blobs // PACK
        self.rows = self.member_row + -(-self.member_rows // 8) * 8
        self.sources, self.edge, self.blobs = sources, edge, blobs

    def pack(self, source_pos, edge_rows, blob_members, counts):
        pieces = [
            source_pos.reshape(-1, LANES),
            edge_rows.astype(jnp.float32).reshape(1, LANES),
            jnp.pad(counts.astype(jnp.float32), (0, LANES - counts.shape[0])).reshape(1, LANES),
            jnp.zeros((self.member_row - self.count_row - 1, LANES), jnp.float32),
            blob_members.astype(jnp.float32).reshape(-1, LANES),
        ]
        return jnp.concatenate(pieces, axis=0)

    def members(self, ref, zone):
        return ref[zone, self.member_row : self.member_row + self.member_rows, :].astype(jnp.int32)

    def edges(self, ref, zone):
        return ref[zone, self.edge_row : self.edge_row + 1, :].astype(jnp.int32)

    def live(self, ref, zone):
        shape = (self.member_rows, LANES)
        lane = lax.broadcasted_iota(jnp.int32, shape, 1)
        row = lax.broadcasted_iota(jnp.int32, shape, 0)
        counts = ref[zone, self.count_row : self.count_row + 1, :].astype(jnp.int32)
        held = lane_take(counts, row * PACK + lane // MAX_SOURCES)
        return (lane % MAX_SOURCES) < held


def resolve(cat, zones, cat_ref, edge_ref, table_ref):
    def edge_body(zone, carry):
        index = jnp.broadcast_to(cat.edges(cat_ref, zone), (8, LANES))
        for coord in range(2):
            rows = [
                cat_ref[zone, coord * cat.parts + part : coord * cat.parts + part + 1, :]
                for part in range(cat.parts)
            ]
            edge_ref[coord, zone] = lookup(rows, index)
        return carry

    lax.fori_loop(0, zones, edge_body, 0)

    def member_body(zone, carry):
        member = cat.members(cat_ref, zone)
        before = jnp.maximum(zone - 1, 0)
        after = jnp.minimum(zone + 1, zones - 1)
        lane = lax.broadcasted_iota(jnp.int32, (8, LANES), 1)
        low = member < cat.edge
        high = member >= cat.edge + cat.sources
        own = jnp.clip(member - cat.edge, 0, cat.sources - 1)
        rim = jnp.where(low, cat.edge + member, jnp.where(high, member - cat.edge - cat.sources, 0))
        start = pl.multiple_of(zone * cat.member_rows, 8)
        for coord in range(2):
            rows = [
                cat_ref[zone, coord * cat.parts + part : coord * cat.parts + part + 1, :]
                for part in range(cat.parts)
            ]
            table = jnp.where(lane >= cat.edge, edge_ref[coord, before], edge_ref[coord, after])
            at_rim = lane_take(table[:1], rim)
            table_ref[coord, pl.ds(start, cat.member_rows), :] = jnp.where(
                low | high, at_rim, lookup(rows, own)
            )
        table_ref[2, pl.ds(start, cat.member_rows), :] = cat.live(cat_ref, zone).astype(jnp.float32)
        return carry

    lax.fori_loop(0, zones, member_body, 0)


def tile_kernel(
    cat, zones, groups,
    blob_ref, band_ref, shift_ref, amp_ref, spread_ref,
    cat_ref, pixel_ref, weight_ref,
    out_ref, edge_ref, table_ref, factor_ref, used_ref,
):
    step = pl.program_id(0)
    height = pixel_ref.shape[1]

    @pl.when(step == 0)
    def _():
        out_ref[...] = jnp.zeros_like(out_ref)
        for zone in range(zones):
            used_ref[zone] = 0
        resolve(cat, zones, cat_ref, edge_ref, table_ref)

    shape = (MAX_SOURCES, LANES)
    lane = lax.broadcasted_iota(jnp.int32, shape, 1)
    sub = lax.broadcasted_iota(jnp.int32, shape, 0)
    lane_f = lane.astype(jnp.float32)
    row_f = (lane % height).astype(jnp.float32)
    comp = lane // height
    upper = sub < 8

    for slot in range(pixel_ref.shape[0]):
        tile = step * pixel_ref.shape[0] + slot
        blob = blob_ref[tile]
        at = blob // PACK
        mine = lane == (blob % PACK) * MAX_SOURCES + sub
        row_pos, col_pos, live = [
            jnp.sum(
                jnp.where(mine, jnp.broadcast_to(table_ref[k, pl.ds(at, 1), :], shape), 0.0),
                axis=1,
                keepdims=True,
            )
            for k in range(3)
        ]
        spread = [spread_ref[g, tile] for g in range(COMPS)]
        amp = [amp_ref[g, tile] for g in range(COMPS)]
        row_spread = jnp.where(comp == 0, spread[0], jnp.where(comp == 1, spread[1], spread[2]))
        row_amp = jnp.where(comp == 0, amp[0], jnp.where(comp == 1, amp[1], amp[2]))
        drow = row_f - shift_ref[0, tile] - row_pos
        rows = jnp.exp(-row_spread * (drow * drow)) * (row_amp * live)
        dcol = lane_f - shift_ref[1, tile] - col_pos
        dcol = dcol * dcol
        cols = [jnp.exp(-spread[g] * dcol) for g in range(COMPS)]
        root = jnp.sqrt(weight_ref[slot])
        image = root * pixel_ref[slot]
        for i in range(height):
            model = rows[:, i : i + 1] * cols[0]
            for g in range(1, COMPS):
                model = model + rows[:, g * height + i : g * height + i + 1] * cols[g]
            scaled = model * root[i : i + 1, :]
            head = scaled.astype(jnp.bfloat16)
            tail = (scaled - head.astype(jnp.float32)).astype(jnp.bfloat16)
            line = jnp.broadcast_to(image[i : i + 1, :], shape)
            line_head = line.astype(jnp.bfloat16).astype(jnp.float32)
            seen = jnp.where(upper, line_head, line - line_head).astype(jnp.bfloat16)
            where = slice(i * LANES, (i + 1) * LANES)
            factor_ref[slot, 0:16, where] = head
            factor_ref[slot, 16:32, where] = tail
            factor_ref[slot, 32:48, where] = seen
        product = lax.dot_general(
            factor_ref[slot],
            factor_ref[slot, 0:32, :],
            (((1,), (1,)), ((), ())),
            preferred_element_type=jnp.float32,
        )
        folded = product[:, :16] + product[:, 16:]
        normal = folded[:16] + folded[16:32]
        vector = folded[32:40] + folded[40:48]
        zone = blob // cat.blobs
        code = band_ref[tile] * cat.blobs + blob % cat.blobs
        eight = lax.broadcasted_iota(jnp.int32, vector.shape, 0)
        tailrows = jnp.where(
            eight == 0, vector, jnp.where(eight == 1, code.astype(jnp.float32), 0.0)
        )
        entry = jnp.concatenate([normal, tailrows], axis=0)
        entry = jnp.concatenate(
            [entry, jnp.zeros((ROWS, LANES - MAX_SOURCES), jnp.float32)], axis=1
        )
        order = used_ref[zone]
        used_ref[zone] = order + 1
        seat = order % PACK
        entry = pltpu.roll(entry, seat * MAX_SOURCES, 1)
        place = zone * groups + order // PACK
        out_ref[place] = out_ref[place] + entry


def tile_terms(cat, zones, groups, blob, band, shift, amp, spread, catalogs, pixels, weights):
    tiles, height, width = pixels.shape
    per = TILES_STEP
    while tiles % per:
        per -= 1
    block = pl.BlockSpec((per, height, width), lambda s: (s, 0, 0))
    return pl.pallas_call(
        functools.partial(tile_kernel, cat, zones, groups),
        grid=(tiles // per,),
        out_shape=jax.ShapeDtypeStruct((zones * groups, ROWS, LANES), jnp.float32),
        in_specs=[SMEM] * 5 + [VMEM, block, block],
        out_specs=pl.BlockSpec((zones * groups, ROWS, LANES), lambda s: (0, 0, 0)),
        scratch_shapes=[
            pltpu.VMEM((2, zones, 8, LANES), jnp.float32),
            pltpu.VMEM((3, zones * cat.member_rows, LANES), jnp.float32),
            pltpu.VMEM((per, 48, height * width), jnp.bfloat16),
            pltpu.SMEM((zones,), jnp.int32),
        ],
        compiler_params=pltpu.CompilerParams(dimension_semantics=("arbitrary",)),
    )(blob, band, shift, amp, spread, catalogs, pixels, weights)


def gather_kernel(capacity, groups, code_ref, got_ref, total_ref):
    total_ref[...] = jnp.zeros_like(total_ref)
    lane = lax.broadcasted_iota(jnp.int32, (ROWS, LANES), 1) // MAX_SOURCES

    def body(group, carry):
        block = got_ref[group]
        for seat in range(min(PACK, capacity)):
            code = code_ref[group, seat]
            to = code % PACK
            moved = pltpu.roll(block, ((to - seat + PACK) % PACK) * MAX_SOURCES, 1)
            place = code // PACK
            total_ref[place] = total_ref[place] + jnp.where(lane == to, moved, 0.0)
        return carry

    lax.fori_loop(0, got_ref.shape[0], body, 0)


def solve_kernel(got_ref, out_ref):
    total = got_ref[0]
    for other in range(1, got_ref.shape[0]):
        total = total + got_ref[other]
    for group in range(total.shape[0]):
        block = total[group]
        row = lax.broadcasted_iota(jnp.int32, (ROWS, LANES), 0)
        lane = lax.broadcasted_iota(jnp.int32, (ROWS, LANES), 1)
        column = lane % MAX_SOURCES
        first = lane - column
        block = block + jnp.where(row == column, PRIOR, 0.0)
        scale = jnp.ones((1, LANES), jnp.float32)
        for k in range(MAX_SOURCES):
            taken = jnp.take_along_axis(block, first + k, axis=1, mode="promise_in_bounds")
            pivot = taken[k : k + 1]
            across = block[k : k + 1]
            scale = jnp.where(column[:1] == k, across, scale)
            ratio = jnp.where(column[:1] == k, 0.0, across / pivot)
            block = block - taken * ratio
        out_ref[group : group + 1, :] = block[MAX_SOURCES : MAX_SOURCES + 1] / scale
    out_ref[total.shape[0] :, :] = jnp.zeros(
        (out_ref.shape[0] - total.shape[0], LANES), jnp.float32
    )


def place_kernel(cat, zones, bands, share, zone_ref, cat_ref, flux_ref, out_ref, pick_ref):
    zone = zone_ref[0]
    edges = cat.edges(cat_ref, zone)
    rows = cat.member_rows
    total = jnp.zeros((16, cat.sources), jnp.float32)
    source = lax.broadcasted_iota(jnp.int32, (cat.sources, LANES), 0)
    for side in range(3):
        near = jnp.clip(zone + side - 1, 0, zones - 1)
        member = cat.members(cat_ref, near)
        live = cat.live(cat_ref, near)
        if side == 0:
            valid = (member >= cat.edge + cat.sources) & (zone > 0)
            target = lane_take(edges, jnp.where(valid, member - cat.edge - cat.sources, 0))
        elif side == 1:
            valid = (member >= cat.edge) & (member < cat.edge + cat.sources)
            target = member - cat.edge
        else:
            valid = (member < cat.edge) & (zone < zones - 1)
            target = lane_take(edges, jnp.where(valid, member + cat.edge, 0))
        valid = valid & live
        target = jnp.where(valid, target, -1)
        parts = []
        for band in range(FILTER_BANDS):
            lines = []
            for row in range(rows):
                group = band * rows + row
                lines.append(flux_ref[side * bands + group // share, group % share : group % share + 1, :])
            parts.append(jnp.concatenate(lines, axis=1))
        values = jnp.concatenate(parts, axis=0)
        pieces = []
        for _ in range(3):
            piece = values.astype(jnp.bfloat16).astype(jnp.float32)
            values = values - piece
            pieces.append(piece)
        pieces.append(jnp.zeros((16 - 3 * FILTER_BANDS, values.shape[1]), jnp.float32))
        left = jnp.concatenate(pieces, axis=0).astype(jnp.bfloat16)
        for row in range(rows):
            hit = source == target[row : row + 1, :]
            pick_ref[:, row * LANES : (row + 1) * LANES] = jnp.where(hit, 1.0, 0.0).astype(jnp.bfloat16)
        total = total + lax.dot_general(
            left, pick_ref[...], (((1,), (1,)), ((), ())), preferred_element_type=jnp.float32
        )
    out_ref[...] = total[0:3] + total[3:6] + total[6:9]


def on_device(
    sizes, pixels, inv_var, tile_offset, psf_amp, psf_sigma, tile_blob, tile_band,
    source_pos, edge_rows, blob_members, sources_per_blob,
):
    zones, bands = sizes
    blobs = sources_per_blob.shape[0]
    sources = source_pos.shape[1]
    tiles = pixels.shape[0]
    cat = Catalog(sources, edge_rows.shape[0] // 2, blobs)
    capacity = max(2, (2 * tiles + zones - 1) // zones)
    groups = -(-capacity // PACK)
    systems = FILTER_BANDS * blobs // PACK
    share = systems // bands
    zone_moves = [(d, 0) for d in range(1, zones)]
    band_moves = [(0, d) for d in range(1, bands)]
    near_moves = [(dz, db) for dz in (-1, 0, 1) for db in range(bands) if dz or db]

    packed = cat.pack(source_pos, edge_rows, blob_members, sources_per_blob)
    catalogs = exchange(packed, zone_moves, None, lambda dz, db, z, b: z, zones, sizes, 0)
    spread = 0.5 / (psf_sigma * psf_sigma)
    terms = tile_terms(
        cat, zones, groups, tile_blob, tile_band, tile_offset, psf_amp, spread, catalogs,
        pixels, inv_var,
    )
    got = exchange(
        terms.reshape(zones, groups * ROWS, LANES),
        zone_moves, lambda z, b: z, lambda dz, db, z, b: z, zones, sizes, 1,
    ).reshape(zones * groups, ROWS, LANES)
    codes = got[:, MAX_SOURCES + 1, ::MAX_SOURCES].astype(jnp.int32)
    totals = pl.pallas_call(
        functools.partial(gather_kernel, capacity, groups),
        out_shape=jax.ShapeDtypeStruct((systems, ROWS, LANES), jnp.float32),
        in_specs=[SMEM, VMEM],
        out_specs=VMEM,
    )(codes, got)
    shares = exchange(
        totals.reshape(bands, share * ROWS, LANES),
        band_moves, lambda z, b: b, lambda dz, db, z, b: b, bands, sizes, 2,
    )
    solved = pl.pallas_call(
        solve_kernel,
        out_shape=jax.ShapeDtypeStruct((-(-share // 8) * 8, LANES), jnp.float32),
        in_specs=[VMEM],
        out_specs=VMEM,
    )(shares.reshape(bands, share, ROWS, LANES))
    fluxes = exchange(
        solved, near_moves, None, lambda dz, db, z, b: (1 - dz) * bands + b, 3 * bands, sizes, 3
    )
    return pl.pallas_call(
        functools.partial(place_kernel, cat, zones, bands, share),
        out_shape=jax.ShapeDtypeStruct((FILTER_BANDS, sources), jnp.float32),
        in_specs=[SMEM, VMEM, VMEM],
        out_specs=VMEM,
        scratch_shapes=[pltpu.VMEM((sources, cat.member_rows * LANES), jnp.bfloat16)],
    )(lax.axis_index("zone").reshape(1), catalogs, fluxes)


def solution(mesh):
    sizes = (mesh.shape["zone"], mesh.shape["band"])
    return jax.shard_map(
        functools.partial(on_device, sizes),
        mesh=mesh,
        in_specs=(
            P(("zone", "band"), None, None),
            P(("zone", "band"), None, None),
            P(None, ("zone", "band")),
            P(None, ("zone", "band")),
            P(None, ("zone", "band")),
            P(("zone", "band")),
            P(("zone", "band")),
            P(None, "zone"),
            P("zone"),
            P("zone", None),
            P("zone"),
        ),
        out_specs=P(None, "zone"),
        check_vma=False,
    )
```

```python
import functools

import jax
import jax.numpy as jnp
from jax import lax
from jax.experimental import pallas as pl
from jax.experimental.pallas import tpu as pltpu
from jax.sharding import PartitionSpec as P

FILTER_BANDS = 3
COMPS = 3
MAX_SOURCES = 16
LANES = 128
PACK = LANES // MAX_SOURCES
ROWS = 24
TILES_STEP = 4
PRIOR = 1.0

VMEM = pl.BlockSpec(memory_space=pltpu.VMEM)
SMEM = pl.BlockSpec(memory_space=pltpu.SMEM)


def exchange(block, moves, pick, slot, slots, sizes, ident):
    zones, bands = sizes
    piece = block.shape[-2:] if pick is None else block.shape[1:]

    def kernel(x_ref, o_ref, send_sem, recv_sem, own_sem):
        zone = lax.axis_index("zone")
        band = lax.axis_index("band")
        targets = [
            (lax.rem(zone + dz + zones, zones), lax.rem(band + db + bands, bands))
            for dz, db in moves
        ]
        barrier = pltpu.get_barrier_semaphore()
        for target in targets:
            pl.semaphore_signal(
                barrier, inc=1, device_id=target, device_id_type=pl.DeviceIdType.MESH
            )
        own_src = x_ref if pick is None else x_ref.at[pick(zone, band)]
        own = pltpu.make_async_copy(own_src, o_ref.at[slot(0, 0, zone, band)], own_sem)
        own.start()
        pl.semaphore_wait(barrier, len(moves))
        copies = []
        for order, ((dz, db), target) in enumerate(zip(moves, targets)):
            copy = pltpu.make_async_remote_copy(
                src_ref=x_ref if pick is None else x_ref.at[pick(*target)],
                dst_ref=o_ref.at[slot(dz, db, zone, band)],
                send_sem=send_sem.at[order],
                recv_sem=recv_sem.at[order],
                device_id=target,
                device_id_type=pl.DeviceIdType.MESH,
            )
            copy.start()
            copies.append(copy)
        own.wait()
        for copy in copies:
            copy.wait()

    return pl.pallas_call(
        kernel,
        out_shape=jax.ShapeDtypeStruct((slots,) + piece, block.dtype),
        in_specs=[VMEM],
        out_specs=VMEM,
        scratch_shapes=[
            pltpu.SemaphoreType.DMA((len(moves),)),
            pltpu.SemaphoreType.DMA((len(moves),)),
            pltpu.SemaphoreType.DMA,
        ],
        compiler_params=pltpu.CompilerParams(collective_id=ident, has_side_effects=True),
    )(block)


def lane_take(row, index):
    table = jnp.broadcast_to(row, index.shape)
    return jnp.take_along_axis(table, index, axis=1, mode="promise_in_bounds")


def lookup(rows, index):
    found = jnp.zeros(index.shape, rows[0].dtype)
    low = index & (LANES - 1)
    for part, row in enumerate(rows):
        found = jnp.where(index // LANES == part, lane_take(row, low), found)
    return found


class Catalog:
    def __init__(self, sources, edge, blobs):
        self.parts = sources // LANES
        self.edge_row = 2 * self.parts
        self.count_row = self.edge_row + 1
        self.member_row = -(-(self.count_row + 1) // 8) * 8
        self.member_rows = blobs // PACK
        self.rows = self.member_row + -(-self.member_rows // 8) * 8
        self.sources, self.edge, self.blobs = sources, edge, blobs

    def pack(self, source_pos, edge_rows, blob_members, counts):
        pieces = [
            source_pos.reshape(-1, LANES),
            edge_rows.astype(jnp.float32).reshape(1, LANES),
            jnp.pad(counts.astype(jnp.float32), (0, LANES - counts.shape[0])).reshape(1, LANES),
            jnp.zeros((self.member_row - self.count_row - 1, LANES), jnp.float32),
            blob_members.astype(jnp.float32).reshape(-1, LANES),
        ]
        return jnp.concatenate(pieces, axis=0)

    def members(self, ref, zone):
        return ref[zone, self.member_row : self.member_row + self.member_rows, :].astype(jnp.int32)

    def edges(self, ref, zone):
        return ref[zone, self.edge_row : self.edge_row + 1, :].astype(jnp.int32)

    def live(self, ref, zone):
        shape = (self.member_rows, LANES)
        lane = lax.broadcasted_iota(jnp.int32, shape, 1)
        row = lax.broadcasted_iota(jnp.int32, shape, 0)
        counts = ref[zone, self.count_row : self.count_row + 1, :].astype(jnp.int32)
        held = lane_take(counts, row * PACK + lane // MAX_SOURCES)
        return (lane % MAX_SOURCES) < held


def resolve(cat, zones, cat_ref, edge_ref, table_ref):
    def edge_body(zone, carry):
        index = jnp.broadcast_to(cat.edges(cat_ref, zone), (8, LANES))
        for coord in range(2):
            rows = [
                cat_ref[zone, coord * cat.parts + part : coord * cat.parts + part + 1, :]
                for part in range(cat.parts)
            ]
            edge_ref[coord, zone] = lookup(rows, index)
        return carry

    lax.fori_loop(0, zones, edge_body, 0)

    def member_body(zone, carry):
        member = cat.members(cat_ref, zone)
        before = jnp.maximum(zone - 1, 0)
        after = jnp.minimum(zone + 1, zones - 1)
        lane = lax.broadcasted_iota(jnp.int32, (8, LANES), 1)
        low = member < cat.edge
        high = member >= cat.edge + cat.sources
        own = jnp.clip(member - cat.edge, 0, cat.sources - 1)
        rim = jnp.where(low, cat.edge + member, jnp.where(high, member - cat.edge - cat.sources, 0))
        start = pl.multiple_of(zone * cat.member_rows, 8)
        for coord in range(2):
            rows = [
                cat_ref[zone, coord * cat.parts + part : coord * cat.parts + part + 1, :]
                for part in range(cat.parts)
            ]
            table = jnp.where(lane >= cat.edge, edge_ref[coord, before], edge_ref[coord, after])
            at_rim = lane_take(table[:1], rim)
            table_ref[coord, pl.ds(start, cat.member_rows), :] = jnp.where(
                low | high, at_rim, lookup(rows, own)
            )
        table_ref[2, pl.ds(start, cat.member_rows), :] = cat.live(cat_ref, zone).astype(jnp.float32)
        return carry

    lax.fori_loop(0, zones, member_body, 0)


def tile_kernel(
    cat, zones, groups,
    blob_ref, band_ref, shift_ref, amp_ref, spread_ref,
    cat_ref, pixel_ref, weight_ref,
    out_ref, edge_ref, table_ref, factor_ref, line_ref, used_ref,
):
    step = pl.program_id(0)
    height = pixel_ref.shape[1]

    @pl.when(step == 0)
    def _():
        out_ref[...] = jnp.zeros_like(out_ref)
        for zone in range(zones):
            used_ref[zone] = 0
        resolve(cat, zones, cat_ref, edge_ref, table_ref)

    half = MAX_SOURCES // 2
    shape = (MAX_SOURCES, LANES)
    lane = lax.broadcasted_iota(jnp.int32, shape, 1)
    sub = lax.broadcasted_iota(jnp.int32, shape, 0)
    lane_f = lane.astype(jnp.float32)
    keep = (lane % half) == (sub % half)
    tall = (height, LANES)
    tall_lane = lax.broadcasted_iota(jnp.int32, tall, 1)
    row_f = lax.broadcasted_iota(jnp.int32, tall, 0).astype(jnp.float32)
    eight_lane = tall_lane[:8]
    comp = (eight_lane[:1] // half) % COMPS
    width = COMPS * half
    high_part = (tall_lane < width) | (tall_lane >= 2 * width)
    used_part = tall_lane < 3 * width
    blank = jnp.zeros((LANES - 3 * width, LANES), jnp.float32)

    for slot in range(pixel_ref.shape[0]):
        tile = step * pixel_ref.shape[0] + slot
        blob = blob_ref[tile]
        at = blob // PACK
        offset = (blob % PACK) * MAX_SOURCES
        table = [
            jnp.broadcast_to(table_ref[k, pl.ds(at, 1), :], shape) for k in range(3)
        ]
        col_pos = jnp.sum(
            jnp.where(lane == offset + sub, table[1], 0.0), axis=1, keepdims=True
        )
        spread = [spread_ref[g, tile] for g in range(COMPS)]
        amp = [amp_ref[g, tile] for g in range(COMPS)]
        row_spread = jnp.where(comp == 0, spread[0], jnp.where(comp == 1, spread[1], spread[2]))
        row_amp = jnp.where(comp == 0, amp[0], jnp.where(comp == 1, amp[1], amp[2]))
        dcol = lane_f - shift_ref[1, tile] - col_pos
        dcol = dcol * dcol
        cols = [jnp.exp(-spread[g] * dcol) for g in range(COMPS)]
        cols_head = [col.astype(jnp.bfloat16).astype(jnp.float32) for col in cols]
        cols_tail = [col - head for col, head in zip(cols, cols_head)]
        root = jnp.sqrt(weight_ref[slot])
        image = root * pixel_ref[slot]
        image_head = image.astype(jnp.bfloat16).astype(jnp.float32)
        line_ref[slot, 0] = root
        line_ref[slot, 1] = image_head
        line_ref[slot, 2] = image - image_head
        models = []
        for h in range(2):
            index = offset + h * half + eight_lane % half
            row_pos = jnp.take_along_axis(table[0][:8], index, axis=1, mode="promise_in_bounds")
            live = jnp.take_along_axis(table[2][:8], index, axis=1, mode="promise_in_bounds")
            drow = row_f - shift_ref[0, tile] - row_pos[:1]
            rows = jnp.exp(-row_spread * (drow * drow)) * (row_amp * live[:1])
            rows_head = rows.astype(jnp.bfloat16).astype(jnp.float32)
            line_ref[slot, 3 + h] = jnp.where(
                used_part, jnp.where(high_part, rows_head, rows - rows_head), 0.0
            )
            span = slice(h * half, (h + 1) * half)
            heads = [c[span] for c in cols_head]
            right = jnp.concatenate(
                heads + heads + [c[span] for c in cols_tail] + [blank], axis=0
            ).astype(jnp.bfloat16)
            left = []
            for i in range(0, height, 2):
                pair = jnp.concatenate(
                    [
                        jnp.broadcast_to(line_ref[slot, 3 + h, i + d : i + d + 1, :], (half, LANES))
                        for d in range(2)
                    ],
                    axis=0,
                )
                left.append(jnp.where(keep, pair, 0.0).astype(jnp.bfloat16))
            models.append(
                lax.dot_general(
                    jnp.concatenate(left, axis=0), right, (((1,), (0,)), ((), ())),
                    preferred_element_type=jnp.float32,
                )
            )
        for i in range(height):
            span = slice(i * half, (i + 1) * half)
            weight = jnp.broadcast_to(line_ref[slot, 0, i : i + 1, :], shape)
            scaled = jnp.concatenate([models[0][span], models[1][span]], axis=0) * weight
            head = scaled.astype(jnp.bfloat16)
            tail = (scaled - head.astype(jnp.float32)).astype(jnp.bfloat16)
            seen = jnp.concatenate(
                [
                    jnp.broadcast_to(line_ref[slot, k, i : i + 1, :], (half, LANES))
                    for k in (1, 2)
                ],
                axis=0,
            ).astype(jnp.bfloat16)
            where = slice(i * LANES, (i + 1) * LANES)
            factor_ref[slot, 0:16, where] = head
            factor_ref[slot, 16:32, where] = tail
            factor_ref[slot, 32:48, where] = seen
        product = lax.dot_general(
            factor_ref[slot],
            factor_ref[slot, 0:32, :],
            (((1,), (1,)), ((), ())),
            preferred_element_type=jnp.float32,
        )
        folded = product[:, :16] + product[:, 16:]
        normal = folded[:16] + folded[16:32]
        vector = folded[32:40] + folded[40:48]
        zone = blob // cat.blobs
        code = band_ref[tile] * cat.blobs + blob % cat.blobs
        eight = lax.broadcasted_iota(jnp.int32, vector.shape, 0)
        tailrows = jnp.where(
            eight == 0, vector, jnp.where(eight == 1, code.astype(jnp.float32), 0.0)
        )
        entry = jnp.concatenate([normal, tailrows], axis=0)
        entry = jnp.concatenate(
            [entry, jnp.zeros((ROWS, LANES - MAX_SOURCES), jnp.float32)], axis=1
        )
        order = used_ref[zone]
        used_ref[zone] = order + 1
        seat = order % PACK
        entry = pltpu.roll(entry, seat * MAX_SOURCES, 1)
        place = zone * groups + order // PACK
        out_ref[place] = out_ref[place] + entry


def tile_terms(cat, zones, groups, blob, band, shift, amp, spread, catalogs, pixels, weights):
    tiles, height, width = pixels.shape
    per = TILES_STEP
    while tiles % per:
        per -= 1
    block = pl.BlockSpec((per, height, width), lambda s: (s, 0, 0))
    return pl.pallas_call(
        functools.partial(tile_kernel, cat, zones, groups),
        grid=(tiles // per,),
        out_shape=jax.ShapeDtypeStruct((zones * groups, ROWS, LANES), jnp.float32),
        in_specs=[SMEM] * 5 + [VMEM, block, block],
        out_specs=pl.BlockSpec((zones * groups, ROWS, LANES), lambda s: (0, 0, 0)),
        scratch_shapes=[
            pltpu.VMEM((2, zones, 8, LANES), jnp.float32),
            pltpu.VMEM((3, zones * cat.member_rows, LANES), jnp.float32),
            pltpu.VMEM((per, 48, height * width), jnp.bfloat16),
            pltpu.VMEM((per, 5, height, width), jnp.float32),
            pltpu.SMEM((zones,), jnp.int32),
        ],
        compiler_params=pltpu.CompilerParams(dimension_semantics=("arbitrary",)),
    )(blob, band, shift, amp, spread, catalogs, pixels, weights)


def gather_kernel(capacity, groups, code_ref, got_ref, total_ref):
    total_ref[...] = jnp.zeros_like(total_ref)
    lane = lax.broadcasted_iota(jnp.int32, (ROWS, LANES), 1) // MAX_SOURCES

    def body(group, carry):
        block = got_ref[group]
        for seat in range(min(PACK, capacity)):
            code = code_ref[group, seat]
            to = code % PACK
            moved = pltpu.roll(block, ((to - seat + PACK) % PACK) * MAX_SOURCES, 1)
            place = code // PACK
            total_ref[place] = total_ref[place] + jnp.where(lane == to, moved, 0.0)
        return carry

    lax.fori_loop(0, got_ref.shape[0], body, 0)


def solve_group(block):
    row = lax.broadcasted_iota(jnp.int32, (ROWS, LANES), 0)
    lane = lax.broadcasted_iota(jnp.int32, (ROWS, LANES), 1)
    column = lane % MAX_SOURCES
    first = lane - column
    block = block + jnp.where(row == column, PRIOR, 0.0)
    scale = jnp.ones((1, LANES), jnp.float32)
    for k in range(MAX_SOURCES):
        taken = jnp.take_along_axis(block, first + k, axis=1, mode="promise_in_bounds")
        pivot = taken[k : k + 1]
        across = block[k : k + 1]
        scale = jnp.where(column[:1] == k, across, scale)
        ratio = jnp.where(column[:1] == k, 0.0, across / pivot)
        block = block - taken * ratio
    return block[MAX_SOURCES : MAX_SOURCES + 1] / scale


def finish_kernel(
    cat, zones, bands, share, total_ref, cat_ref, out_ref,
    got_ref, solved_ref, flux_ref, pick_ref,
    send_sum, recv_sum, own_sum, send_flux, recv_flux, own_flux,
):
    zone = lax.axis_index("zone")
    band = lax.axis_index("band")
    moves = [(dz, db) for dz in (0, 1, -1) for db in range(bands) if dz or db]
    targets = [
        (lax.rem(zone + dz + zones, zones), lax.rem(band + db, bands)) for dz, db in moves
    ]
    barrier = pltpu.get_barrier_semaphore()
    for target in targets:
        pl.semaphore_signal(barrier, inc=1, device_id=target, device_id_type=pl.DeviceIdType.MESH)
    own = pltpu.make_async_copy(total_ref.at[band], got_ref.at[band], own_sum)
    own.start()
    pl.semaphore_wait(barrier, len(moves))
    sums = []
    for order in range(bands - 1):
        target = targets[order]
        copy = pltpu.make_async_remote_copy(
            src_ref=total_ref.at[target[1]],
            dst_ref=got_ref.at[band],
            send_sem=send_sum.at[order],
            recv_sem=recv_sum.at[order],
            device_id=target,
            device_id_type=pl.DeviceIdType.MESH,
        )
        copy.start()
        sums.append(copy)

    edges = cat.edges(cat_ref, zone)
    rows = cat.member_rows
    source = lax.broadcasted_iota(jnp.int32, (cat.sources, LANES), 0)
    for side in range(3):
        near = lax.rem(zone + side - 1 + zones, zones)
        member = cat.members(cat_ref, near)
        live = cat.live(cat_ref, near)
        if side == 0:
            valid = (member >= cat.edge + cat.sources) & (zone > 0)
            target = lane_take(edges, jnp.where(valid, member - cat.edge - cat.sources, 0))
        elif side == 1:
            valid = (member >= cat.edge) & (member < cat.edge + cat.sources)
            target = member - cat.edge
        else:
            valid = (member < cat.edge) & (zone < zones - 1)
            target = lane_take(edges, jnp.where(valid, member + cat.edge, 0))
        target = jnp.where(valid & live, target, -1)
        for row in range(rows):
            hit = source == target[row : row + 1, :]
            pick_ref[side, :, row * LANES : (row + 1) * LANES] = jnp.where(hit, 1.0, 0.0).astype(
                jnp.bfloat16
            )

    own.wait()
    for copy in sums:
        copy.wait()
    for group in range(share):
        span = slice(group * ROWS, (group + 1) * ROWS)
        block = got_ref[0, span, :]
        for other in range(1, bands):
            block = block + got_ref[other, span, :]
        solved_ref[group : group + 1, :] = solve_group(block)
    if solved_ref.shape[0] > share:
        solved_ref[share:, :] = jnp.zeros((solved_ref.shape[0] - share, LANES), jnp.float32)

    own = pltpu.make_async_copy(solved_ref, flux_ref.at[bands + band], own_flux)
    own.start()
    copies = []
    for order, ((dz, db), target) in enumerate(zip(moves, targets)):
        copy = pltpu.make_async_remote_copy(
            src_ref=solved_ref,
            dst_ref=flux_ref.at[(1 - dz) * bands + band],
            send_sem=send_flux.at[order],
            recv_sem=recv_flux.at[order],
            device_id=target,
            device_id_type=pl.DeviceIdType.MESH,
        )
        copy.start()
        copies.append(copy)
    own.wait()
    for copy in copies:
        copy.wait()

    total = jnp.zeros((16, cat.sources), jnp.float32)
    for side in range(3):
        parts = []
        for band_row in range(FILTER_BANDS):
            lines = []
            for row in range(rows):
                group = band_row * rows + row
                at = group % share
                lines.append(flux_ref[side * bands + group // share, at : at + 1, :])
            parts.append(jnp.concatenate(lines, axis=1))
        values = jnp.concatenate(parts, axis=0)
        pieces = []
        for _ in range(3):
            piece = values.astype(jnp.bfloat16).astype(jnp.float32)
            values = values - piece
            pieces.append(piece)
        pieces.append(jnp.zeros((16 - 3 * FILTER_BANDS, values.shape[1]), jnp.float32))
        left = jnp.concatenate(pieces, axis=0).astype(jnp.bfloat16)
        total = total + lax.dot_general(
            left, pick_ref[side], (((1,), (1,)), ((), ())), preferred_element_type=jnp.float32
        )
    out_ref[...] = total[0:3] + total[3:6] + total[6:9]


def on_device(
    sizes, pixels, inv_var, tile_offset, psf_amp, psf_sigma, tile_blob, tile_band,
    source_pos, edge_rows, blob_members, sources_per_blob,
):
    zones, bands = sizes
    blobs = sources_per_blob.shape[0]
    sources = source_pos.shape[1]
    tiles = pixels.shape[0]
    cat = Catalog(sources, edge_rows.shape[0] // 2, blobs)
    capacity = max(2, (2 * tiles + zones - 1) // zones)
    groups = -(-capacity // PACK)
    systems = FILTER_BANDS * blobs // PACK
    share = systems // bands
    zone_moves = [(d, 0) for d in range(1, zones)]

    packed = cat.pack(source_pos, edge_rows, blob_members, sources_per_blob)
    catalogs = exchange(packed, zone_moves, None, lambda dz, db, z, b: z, zones, sizes, 0)
    spread = 0.5 / (psf_sigma * psf_sigma)
    terms = tile_terms(
        cat, zones, groups, tile_blob, tile_band, tile_offset, psf_amp, spread, catalogs,
        pixels, inv_var,
    )
    got = exchange(
        terms.reshape(zones, groups * ROWS, LANES),
        zone_moves, lambda z, b: z, lambda dz, db, z, b: z, zones, sizes, 1,
    ).reshape(zones * groups, ROWS, LANES)
    codes = got[:, MAX_SOURCES + 1, ::MAX_SOURCES].astype(jnp.int32)
    totals = pl.pallas_call(
        functools.partial(gather_kernel, capacity, groups),
        out_shape=jax.ShapeDtypeStruct((systems, ROWS, LANES), jnp.float32),
        in_specs=[SMEM, VMEM],
        out_specs=VMEM,
    )(codes, got)
    near = 3 * bands - 1
    seats = -(-share // 8) * 8
    return pl.pallas_call(
        functools.partial(finish_kernel, cat, zones, bands, share),
        out_shape=jax.ShapeDtypeStruct((FILTER_BANDS, sources), jnp.float32),
        in_specs=[VMEM, VMEM],
        out_specs=VMEM,
        scratch_shapes=[
            pltpu.VMEM((bands, share * ROWS, LANES), jnp.float32),
            pltpu.VMEM((seats, LANES), jnp.float32),
            pltpu.VMEM((3 * bands, seats, LANES), jnp.float32),
            pltpu.VMEM((3, sources, cat.member_rows * LANES), jnp.bfloat16),
            pltpu.SemaphoreType.DMA((bands - 1,)),
            pltpu.SemaphoreType.DMA((bands - 1,)),
            pltpu.SemaphoreType.DMA,
            pltpu.SemaphoreType.DMA((near,)),
            pltpu.SemaphoreType.DMA((near,)),
            pltpu.SemaphoreType.DMA,
        ],
        compiler_params=pltpu.CompilerParams(collective_id=2, has_side_effects=True),
    )(totals.reshape(bands, share * ROWS, LANES), catalogs)


def solution(mesh):
    sizes = (mesh.shape["zone"], mesh.shape["band"])
    return jax.shard_map(
        functools.partial(on_device, sizes),
        mesh=mesh,
        in_specs=(
            P(("zone", "band"), None, None),
            P(("zone", "band"), None, None),
            P(None, ("zone", "band")),
            P(None, ("zone", "band")),
            P(None, ("zone", "band")),
            P(("zone", "band")),
            P(("zone", "band")),
            P(None, "zone"),
            P("zone"),
            P("zone", None),
            P("zone"),
        ),
        out_specs=P(None, "zone"),
        check_vma=False,
    )
```

```python
import functools

import jax
import jax.numpy as jnp
from jax import lax
from jax.experimental import pallas as pl
from jax.experimental.pallas import tpu as pltpu
from jax.sharding import PartitionSpec as P

FILTER_BANDS = 3
COMPS = 3
MAX_SOURCES = 16
LANES = 128
PACK = LANES // MAX_SOURCES
ROWS = 24
TILES_STEP = 4
CHUNK = 8
PRIOR = 1.0

VMEM = pl.BlockSpec(memory_space=pltpu.VMEM)
SMEM = pl.BlockSpec(memory_space=pltpu.SMEM)


def exchange(block, moves, pick, slot, slots, sizes, ident, label_row=None):
    zones, bands = sizes
    piece = block.shape[-2:] if pick is None else block.shape[1:]

    def kernel(x_ref, o_ref, *refs):
        send_sem, recv_sem, own_sem = refs[-3:]
        zone = lax.axis_index("zone")
        band = lax.axis_index("band")
        targets = [
            (lax.rem(zone + dz + zones, zones), lax.rem(band + db + bands, bands))
            for dz, db in moves
        ]
        barrier = pltpu.get_barrier_semaphore()
        for target in targets:
            pl.semaphore_signal(
                barrier, inc=1, device_id=target, device_id_type=pl.DeviceIdType.MESH
            )
        own_src = x_ref if pick is None else x_ref.at[pick(zone, band)]
        own = pltpu.make_async_copy(own_src, o_ref.at[slot(0, 0, zone, band)], own_sem)
        own.start()
        pl.semaphore_wait(barrier, len(moves))
        copies = []
        for order, ((dz, db), target) in enumerate(zip(moves, targets)):
            copy = pltpu.make_async_remote_copy(
                src_ref=x_ref if pick is None else x_ref.at[pick(*target)],
                dst_ref=o_ref.at[slot(dz, db, zone, band)],
                send_sem=send_sem.at[order],
                recv_sem=recv_sem.at[order],
                device_id=target,
                device_id_type=pl.DeviceIdType.MESH,
            )
            copy.start()
            copies.append(copy)
        own.wait()
        for copy in copies:
            copy.wait()
        if label_row is not None:
            code_ref = refs[0]
            groups = piece[0] // ROWS
            for order in range(slots * groups):
                at = order % groups * ROWS + label_row
                code_ref[order : order + 1, :] = o_ref[order // groups, at : at + 1, :].astype(
                    jnp.int32
                )

    out_shape = [jax.ShapeDtypeStruct((slots,) + piece, block.dtype)]
    if label_row is not None:
        out_shape.append(jax.ShapeDtypeStruct((slots * piece[0] // ROWS, LANES), jnp.int32))
    return pl.pallas_call(
        kernel,
        out_shape=out_shape,
        in_specs=[VMEM],
        out_specs=[VMEM] * len(out_shape),
        scratch_shapes=[
            pltpu.SemaphoreType.DMA((len(moves),)),
            pltpu.SemaphoreType.DMA((len(moves),)),
            pltpu.SemaphoreType.DMA,
        ],
        compiler_params=pltpu.CompilerParams(collective_id=ident, has_side_effects=True),
    )(block)


def lane_take(row, index):
    table = jnp.broadcast_to(row, index.shape)
    return jnp.take_along_axis(table, index, axis=1, mode="promise_in_bounds")


def lookup(rows, index):
    found = jnp.zeros(index.shape, rows[0].dtype)
    low = index & (LANES - 1)
    for part, row in enumerate(rows):
        found = jnp.where(index // LANES == part, lane_take(row, low), found)
    return found


class Catalog:
    def __init__(self, sources, edge, blobs):
        self.parts = sources // LANES
        self.edge_row = 2 * self.parts
        self.count_row = self.edge_row + 1
        self.member_row = -(-(self.count_row + 1) // 8) * 8
        self.member_rows = blobs // PACK
        self.rows = self.member_row + -(-self.member_rows // 8) * 8
        self.sources, self.edge, self.blobs = sources, edge, blobs

    def pack(self, source_ref, edge_ref, member_ref, count_ref, sigma_ref, out_ref, spread_ref):
        out_ref[...] = jnp.zeros_like(out_ref)
        for coord in range(2):
            for part in range(self.parts):
                at = coord * self.parts + part
                out_ref[at : at + 1, :] = source_ref[
                    coord : coord + 1, part * LANES : (part + 1) * LANES
                ]
        out_ref[self.edge_row : self.edge_row + 1, :] = edge_ref[...].astype(jnp.float32)
        out_ref[self.count_row : self.count_row + 1, : self.blobs] = count_ref[...].astype(
            jnp.float32
        )
        seats = [
            member_ref[pl.ds(seat, self.member_rows, stride=PACK), :].astype(jnp.float32)
            for seat in range(PACK)
        ]
        out_ref[self.member_row : self.member_row + self.member_rows, :] = jnp.concatenate(
            seats, axis=1
        )
        sigma = sigma_ref[...]
        spread_ref[...] = 0.5 / (sigma * sigma)

    def members(self, ref, zone):
        return ref[zone, self.member_row : self.member_row + self.member_rows, :].astype(jnp.int32)

    def edges(self, ref, zone):
        return ref[zone, self.edge_row : self.edge_row + 1, :].astype(jnp.int32)

    def live(self, ref, zone):
        shape = (self.member_rows, LANES)
        lane = lax.broadcasted_iota(jnp.int32, shape, 1)
        row = lax.broadcasted_iota(jnp.int32, shape, 0)
        counts = ref[zone, self.count_row : self.count_row + 1, :].astype(jnp.int32)
        held = lane_take(counts, row * PACK + lane // MAX_SOURCES)
        return (lane % MAX_SOURCES) < held


def resolve(cat, zones, cat_ref, edge_ref, table_ref):
    def edge_body(zone, carry):
        index = jnp.broadcast_to(cat.edges(cat_ref, zone), (8, LANES))
        for coord in range(2):
            rows = [
                cat_ref[zone, coord * cat.parts + part : coord * cat.parts + part + 1, :]
                for part in range(cat.parts)
            ]
            edge_ref[coord, zone] = lookup(rows, index)
        return carry

    lax.fori_loop(0, zones, edge_body, 0)

    def member_body(zone, carry):
        member = cat.members(cat_ref, zone)
        before = jnp.maximum(zone - 1, 0)
        after = jnp.minimum(zone + 1, zones - 1)
        lane = lax.broadcasted_iota(jnp.int32, (8, LANES), 1)
        low = member < cat.edge
        high = member >= cat.edge + cat.sources
        own = jnp.clip(member - cat.edge, 0, cat.sources - 1)
        rim = jnp.where(low, cat.edge + member, jnp.where(high, member - cat.edge - cat.sources, 0))
        start = pl.multiple_of(zone * cat.member_rows, 8)
        for coord in range(2):
            rows = [
                cat_ref[zone, coord * cat.parts + part : coord * cat.parts + part + 1, :]
                for part in range(cat.parts)
            ]
            table = jnp.where(lane >= cat.edge, edge_ref[coord, before], edge_ref[coord, after])
            at_rim = lane_take(table[:1], rim)
            table_ref[coord, pl.ds(start, cat.member_rows), :] = jnp.where(
                low | high, at_rim, lookup(rows, own)
            )
        table_ref[2, pl.ds(start, cat.member_rows), :] = cat.live(cat_ref, zone).astype(jnp.float32)
        return carry

    lax.fori_loop(0, zones, member_body, 0)


def tile_kernel(
    cat, zones, groups,
    blob_ref, band_ref, shift_ref, amp_ref, spread_ref,
    cat_ref, pixel_ref, weight_ref,
    out_ref, edge_ref, table_ref, line_ref, used_ref,
):
    step = pl.program_id(0)
    height = pixel_ref.shape[1]

    @pl.when(step == 0)
    def _():
        out_ref[...] = jnp.zeros_like(out_ref)
        for zone in range(zones):
            used_ref[zone] = 0
        resolve(cat, zones, cat_ref, edge_ref, table_ref)

    half = MAX_SOURCES // 2
    shape = (MAX_SOURCES, LANES)
    lane = lax.broadcasted_iota(jnp.int32, shape, 1)
    sub = lax.broadcasted_iota(jnp.int32, shape, 0)
    lane_f = lane.astype(jnp.float32)
    keep = (lane % half) == (sub % half)
    tall = (height, LANES)
    tall_lane = lax.broadcasted_iota(jnp.int32, tall, 1)
    row_f = lax.broadcasted_iota(jnp.int32, tall, 0).astype(jnp.float32)
    eight_lane = tall_lane[:8]
    comp = (eight_lane[:1] // half) % COMPS
    width = COMPS * half
    high_part = (tall_lane < width) | (tall_lane >= 2 * width)
    used_part = tall_lane < 3 * width
    blank = jnp.zeros((LANES - 3 * width, LANES), jnp.float32)

    for slot in range(pixel_ref.shape[0]):
        tile = step * pixel_ref.shape[0] + slot
        blob = blob_ref[tile]
        at = blob // PACK
        offset = (blob % PACK) * MAX_SOURCES
        table = [
            jnp.broadcast_to(table_ref[k, pl.ds(at, 1), :], shape) for k in range(3)
        ]
        col_pos = jnp.sum(
            jnp.where(lane == offset + sub, table[1], 0.0), axis=1, keepdims=True
        )
        spread = [spread_ref[g, tile] for g in range(COMPS)]
        amp = [amp_ref[g, tile] for g in range(COMPS)]
        row_spread = jnp.where(comp == 0, spread[0], jnp.where(comp == 1, spread[1], spread[2]))
        row_amp = jnp.where(comp == 0, amp[0], jnp.where(comp == 1, amp[1], amp[2]))
        dcol = lane_f - shift_ref[1, tile] - col_pos
        dcol = dcol * dcol
        cols = [jnp.exp(-spread[g] * dcol) for g in range(COMPS)]
        cols_head = [col.astype(jnp.bfloat16).astype(jnp.float32) for col in cols]
        cols_tail = [col - head for col, head in zip(cols, cols_head)]
        root = jnp.sqrt(weight_ref[slot])
        image = root * pixel_ref[slot]
        image_head = image.astype(jnp.bfloat16).astype(jnp.float32)
        line_ref[slot, 0] = root
        line_ref[slot, 1] = image_head
        line_ref[slot, 2] = image - image_head
        rights = []
        for h in range(2):
            index = offset + h * half + eight_lane % half
            row_pos = jnp.take_along_axis(table[0][:8], index, axis=1, mode="promise_in_bounds")
            live = jnp.take_along_axis(table[2][:8], index, axis=1, mode="promise_in_bounds")
            drow = row_f - shift_ref[0, tile] - row_pos[:1]
            rows = jnp.exp(-row_spread * (drow * drow)) * (row_amp * live[:1])
            rows_head = rows.astype(jnp.bfloat16).astype(jnp.float32)
            line_ref[slot, 3 + h] = jnp.where(
                used_part, jnp.where(high_part, rows_head, rows - rows_head), 0.0
            )
            span = slice(h * half, (h + 1) * half)
            heads = [c[span] for c in cols_head]
            rights.append(
                jnp.concatenate(
                    heads + heads + [c[span] for c in cols_tail] + [blank], axis=0
                ).astype(jnp.bfloat16)
            )

        def render(chunk):
            models = []
            for h in range(2):
                left = []
                for i in range(chunk * CHUNK, (chunk + 1) * CHUNK, 2):
                    pair = jnp.concatenate(
                        [
                            jnp.broadcast_to(
                                line_ref[slot, 3 + h, i + d : i + d + 1, :], (half, LANES)
                            )
                            for d in range(2)
                        ],
                        axis=0,
                    )
                    left.append(jnp.where(keep, pair, 0.0).astype(jnp.bfloat16))
                models.append(
                    lax.dot_general(
                        jnp.concatenate(left, axis=0), rights[h], (((1,), (0,)), ((), ())),
                        preferred_element_type=jnp.float32,
                    )
                )
            return models

        product = None
        chunks = height // CHUNK
        ahead = render(0)
        for chunk in range(chunks):
            models = ahead
            if chunk + 1 < chunks:
                ahead = render(chunk + 1)
            heads, tails, lines = [], [], []
            for at_row in range(CHUNK):
                i = chunk * CHUNK + at_row
                span = slice(at_row * half, (at_row + 1) * half)
                weight = jnp.broadcast_to(line_ref[slot, 0, i : i + 1, :], shape)
                scaled = jnp.concatenate([models[0][span], models[1][span]], axis=0) * weight
                head = scaled.astype(jnp.bfloat16)
                heads.append(head)
                tails.append((scaled - head.astype(jnp.float32)).astype(jnp.bfloat16))
                lines.append(
                    jnp.concatenate(
                        [
                            jnp.broadcast_to(line_ref[slot, k, i : i + 1, :], (half, LANES))
                            for k in (1, 2)
                        ],
                        axis=0,
                    ).astype(jnp.bfloat16)
                )
            factor = jnp.concatenate(
                [jnp.concatenate(heads, axis=1), jnp.concatenate(tails, axis=1)], axis=0
            )
            left = jnp.concatenate([factor, jnp.concatenate(lines, axis=1)], axis=0)
            part = lax.dot_general(
                left, factor, (((1,), (1,)), ((), ())), preferred_element_type=jnp.float32
            )
            product = part if product is None else product + part
        folded = product[:, :16] + product[:, 16:]
        normal = folded[:16] + folded[16:32]
        vector = folded[32:40] + folded[40:48]
        zone = blob // cat.blobs
        code = band_ref[tile] * cat.blobs + blob % cat.blobs
        eight = lax.broadcasted_iota(jnp.int32, vector.shape, 0)
        tailrows = jnp.where(
            eight == 0, vector, jnp.where(eight == 1, code.astype(jnp.float32), 0.0)
        )
        entry = jnp.concatenate([normal, tailrows], axis=0)
        entry = jnp.concatenate(
            [entry, jnp.zeros((ROWS, LANES - MAX_SOURCES), jnp.float32)], axis=1
        )
        order = used_ref[zone]
        used_ref[zone] = order + 1
        seat = order % PACK
        entry = pltpu.roll(entry, seat * MAX_SOURCES, 1)
        place = zone * groups + order // PACK
        out_ref[place] = out_ref[place] + entry


def tile_terms(cat, zones, groups, blob, band, shift, amp, spread, catalogs, pixels, weights):
    tiles, height, width = pixels.shape
    per = TILES_STEP
    while tiles % per:
        per -= 1
    block = pl.BlockSpec((per, height, width), lambda s: (s, 0, 0))
    return pl.pallas_call(
        functools.partial(tile_kernel, cat, zones, groups),
        grid=(tiles // per,),
        out_shape=jax.ShapeDtypeStruct((zones * groups, ROWS, LANES), jnp.float32),
        in_specs=[SMEM] * 5 + [VMEM, block, block],
        out_specs=pl.BlockSpec((zones * groups, ROWS, LANES), lambda s: (0, 0, 0)),
        scratch_shapes=[
            pltpu.VMEM((2, zones, 8, LANES), jnp.float32),
            pltpu.VMEM((3, zones * cat.member_rows, LANES), jnp.float32),
            pltpu.VMEM((per, 5, height, width), jnp.float32),
            pltpu.SMEM((zones,), jnp.int32),
        ],
        compiler_params=pltpu.CompilerParams(dimension_semantics=("arbitrary",)),
    )(blob, band, shift, amp, spread, catalogs, pixels, weights)


def gather_kernel(capacity, groups, code_ref, got_ref, total_ref):
    total_ref[...] = jnp.zeros_like(total_ref)
    lane = lax.broadcasted_iota(jnp.int32, (ROWS, LANES), 1) // MAX_SOURCES

    def body(group, carry):
        block = got_ref[group]
        for seat in range(min(PACK, capacity)):
            code = code_ref[group, seat * MAX_SOURCES]
            to = code % PACK
            moved = pltpu.roll(block, ((to - seat + PACK) % PACK) * MAX_SOURCES, 1)
            place = code // PACK
            total_ref[place] = total_ref[place] + jnp.where(lane == to, moved, 0.0)
        return carry

    lax.fori_loop(0, got_ref.shape[0], body, 0)


def solve_group(block):
    row = lax.broadcasted_iota(jnp.int32, (ROWS, LANES), 0)
    lane = lax.broadcasted_iota(jnp.int32, (ROWS, LANES), 1)
    column = lane % MAX_SOURCES
    first = lane - column
    block = block + jnp.where(row == column, PRIOR, 0.0)
    scale = jnp.ones((1, LANES), jnp.float32)
    for k in range(MAX_SOURCES):
        taken = jnp.take_along_axis(block, first + k, axis=1, mode="promise_in_bounds")
        pivot = taken[k : k + 1]
        across = block[k : k + 1]
        scale = jnp.where(column[:1] == k, across, scale)
        ratio = jnp.where(column[:1] == k, 0.0, across / pivot)
        block = block - taken * ratio
    return block[MAX_SOURCES : MAX_SOURCES + 1] / scale


def finish_kernel(
    cat, zones, bands, share, total_ref, cat_ref, out_ref,
    got_ref, solved_ref, flux_ref, pick_ref,
    send_sum, recv_sum, own_sum, send_flux, recv_flux, own_flux,
):
    zone = lax.axis_index("zone")
    band = lax.axis_index("band")
    moves = [(dz, db) for dz in (0, 1, -1) for db in range(bands) if dz or db]
    targets = [
        (lax.rem(zone + dz + zones, zones), lax.rem(band + db, bands)) for dz, db in moves
    ]
    barrier = pltpu.get_barrier_semaphore()
    for target in targets:
        pl.semaphore_signal(barrier, inc=1, device_id=target, device_id_type=pl.DeviceIdType.MESH)
    own = pltpu.make_async_copy(total_ref.at[band], got_ref.at[band], own_sum)
    own.start()
    pl.semaphore_wait(barrier, len(moves))
    sums = []
    for order in range(bands - 1):
        target = targets[order]
        copy = pltpu.make_async_remote_copy(
            src_ref=total_ref.at[target[1]],
            dst_ref=got_ref.at[band],
            send_sem=send_sum.at[order],
            recv_sem=recv_sum.at[order],
            device_id=target,
            device_id_type=pl.DeviceIdType.MESH,
        )
        copy.start()
        sums.append(copy)

    edges = cat.edges(cat_ref, zone)
    rows = cat.member_rows
    source = lax.broadcasted_iota(jnp.int32, (cat.sources, LANES), 0)
    for side in range(3):
        near = lax.rem(zone + side - 1 + zones, zones)
        member = cat.members(cat_ref, near)
        live = cat.live(cat_ref, near)
        if side == 0:
            valid = (member >= cat.edge + cat.sources) & (zone > 0)
            target = lane_take(edges, jnp.where(valid, member - cat.edge - cat.sources, 0))
        elif side == 1:
            valid = (member >= cat.edge) & (member < cat.edge + cat.sources)
            target = member - cat.edge
        else:
            valid = (member < cat.edge) & (zone < zones - 1)
            target = lane_take(edges, jnp.where(valid, member + cat.edge, 0))
        target = jnp.where(valid & live, target, -1)
        for row in range(rows):
            hit = source == target[row : row + 1, :]
            pick_ref[side, :, row * LANES : (row + 1) * LANES] = jnp.where(hit, 1.0, 0.0).astype(
                jnp.bfloat16
            )

    own.wait()
    for copy in sums:
        copy.wait()
    for group in range(share):
        span = slice(group * ROWS, (group + 1) * ROWS)
        block = got_ref[0, span, :]
        for other in range(1, bands):
            block = block + got_ref[other, span, :]
        solved_ref[group : group + 1, :] = solve_group(block)
    if solved_ref.shape[0] > share:
        solved_ref[share:, :] = jnp.zeros((solved_ref.shape[0] - share, LANES), jnp.float32)

    own = pltpu.make_async_copy(solved_ref, flux_ref.at[bands + band], own_flux)
    own.start()
    copies = []
    for order, ((dz, db), target) in enumerate(zip(moves, targets)):
        copy = pltpu.make_async_remote_copy(
            src_ref=solved_ref,
            dst_ref=flux_ref.at[(1 - dz) * bands + band],
            send_sem=send_flux.at[order],
            recv_sem=recv_flux.at[order],
            device_id=target,
            device_id_type=pl.DeviceIdType.MESH,
        )
        copy.start()
        copies.append(copy)
    own.wait()
    for copy in copies:
        copy.wait()

    total = jnp.zeros((16, cat.sources), jnp.float32)
    for side in range(3):
        parts = []
        for band_row in range(FILTER_BANDS):
            lines = []
            for row in range(rows):
                group = band_row * rows + row
                at = group % share
                lines.append(flux_ref[side * bands + group // share, at : at + 1, :])
            parts.append(jnp.concatenate(lines, axis=1))
        values = jnp.concatenate(parts, axis=0)
        pieces = []
        for _ in range(3):
            piece = values.astype(jnp.bfloat16).astype(jnp.float32)
            values = values - piece
            pieces.append(piece)
        pieces.append(jnp.zeros((16 - 3 * FILTER_BANDS, values.shape[1]), jnp.float32))
        left = jnp.concatenate(pieces, axis=0).astype(jnp.bfloat16)
        total = total + lax.dot_general(
            left, pick_ref[side], (((1,), (1,)), ((), ())), preferred_element_type=jnp.float32
        )
    out_ref[...] = total[0:3] + total[3:6] + total[6:9]


def on_device(
    sizes, pixels, inv_var, tile_offset, psf_amp, psf_sigma, tile_blob, tile_band,
    source_pos, edge_rows, blob_members, sources_per_blob,
):
    zones, bands = sizes
    blobs = sources_per_blob.shape[0]
    sources = source_pos.shape[1]
    tiles = pixels.shape[0]
    cat = Catalog(sources, edge_rows.shape[0] // 2, blobs)
    capacity = max(2, (2 * tiles + zones - 1) // zones)
    groups = -(-capacity // PACK)
    systems = FILTER_BANDS * blobs // PACK
    share = systems // bands
    zone_moves = [(d, 0) for d in range(1, zones)]

    packed, spread = pl.pallas_call(
        cat.pack,
        out_shape=(
            jax.ShapeDtypeStruct((cat.rows, LANES), jnp.float32),
            jax.ShapeDtypeStruct(psf_sigma.shape, jnp.float32),
        ),
        in_specs=[VMEM] * 5,
        out_specs=(VMEM, VMEM),
    )(
        source_pos, edge_rows.reshape(1, -1), blob_members, sources_per_blob.reshape(1, -1),
        psf_sigma,
    )
    (catalogs,) = exchange(packed, zone_moves, None, lambda dz, db, z, b: z, zones, sizes, 0)
    terms = tile_terms(
        cat, zones, groups, tile_blob, tile_band, tile_offset, psf_amp, spread, catalogs,
        pixels, inv_var,
    )
    got, codes = exchange(
        terms.reshape(zones, groups * ROWS, LANES),
        zone_moves, lambda z, b: z, lambda dz, db, z, b: z, zones, sizes, 1,
        MAX_SOURCES + 1,
    )
    got = got.reshape(zones * groups, ROWS, LANES)
    totals = pl.pallas_call(
        functools.partial(gather_kernel, capacity, groups),
        out_shape=jax.ShapeDtypeStruct((systems, ROWS, LANES), jnp.float32),
        in_specs=[SMEM, VMEM],
        out_specs=VMEM,
    )(codes, got)
    near = 3 * bands - 1
    seats = -(-share // 8) * 8
    return pl.pallas_call(
        functools.partial(finish_kernel, cat, zones, bands, share),
        out_shape=jax.ShapeDtypeStruct((FILTER_BANDS, sources), jnp.float32),
        in_specs=[VMEM, VMEM],
        out_specs=VMEM,
        scratch_shapes=[
            pltpu.VMEM((bands, share * ROWS, LANES), jnp.float32),
            pltpu.VMEM((seats, LANES), jnp.float32),
            pltpu.VMEM((3 * bands, seats, LANES), jnp.float32),
            pltpu.VMEM((3, sources, cat.member_rows * LANES), jnp.bfloat16),
            pltpu.SemaphoreType.DMA((bands - 1,)),
            pltpu.SemaphoreType.DMA((bands - 1,)),
            pltpu.SemaphoreType.DMA,
            pltpu.SemaphoreType.DMA((near,)),
            pltpu.SemaphoreType.DMA((near,)),
            pltpu.SemaphoreType.DMA,
        ],
        compiler_params=pltpu.CompilerParams(collective_id=2, has_side_effects=True),
    )(totals.reshape(bands, share * ROWS, LANES), catalogs)


def solution(mesh):
    sizes = (mesh.shape["zone"], mesh.shape["band"])
    return jax.shard_map(
        functools.partial(on_device, sizes),
        mesh=mesh,
        in_specs=(
            P(("zone", "band"), None, None),
            P(("zone", "band"), None, None),
            P(None, ("zone", "band")),
            P(None, ("zone", "band")),
            P(None, ("zone", "band")),
            P(("zone", "band")),
            P(("zone", "band")),
            P(None, "zone"),
            P("zone"),
            P("zone", None),
            P("zone"),
        ),
        out_specs=P(None, "zone"),
        check_vma=False,
    )
```

```python
import functools

import jax
import jax.numpy as jnp
from jax import lax
from jax.experimental import pallas as pl
from jax.experimental.pallas import tpu as pltpu
from jax.sharding import PartitionSpec as P

FILTER_BANDS = 3
COMPS = 3
MAX_SOURCES = 16
LANES = 128
PACK = LANES // MAX_SOURCES
ROWS = 24
TILES_STEP = 16
CHUNK = 32
PRIOR = 1.0

VMEM = pl.BlockSpec(memory_space=pltpu.VMEM)
SMEM = pl.BlockSpec(memory_space=pltpu.SMEM)


def exchange(block, moves, pick, slot, slots, sizes, ident, label_row=None):
    zones, bands = sizes
    piece = block.shape[-2:] if pick is None else block.shape[1:]

    def kernel(x_ref, o_ref, *refs):
        send_sem, recv_sem, own_sem = refs[-3:]
        zone = lax.axis_index("zone")
        band = lax.axis_index("band")
        targets = [
            (lax.rem(zone + dz + zones, zones), lax.rem(band + db + bands, bands))
            for dz, db in moves
        ]
        barrier = pltpu.get_barrier_semaphore()
        for target in targets:
            pl.semaphore_signal(
                barrier, inc=1, device_id=target, device_id_type=pl.DeviceIdType.MESH
            )
        own_src = x_ref if pick is None else x_ref.at[pick(zone, band)]
        own = pltpu.make_async_copy(own_src, o_ref.at[slot(0, 0, zone, band)], own_sem)
        own.start()
        pl.semaphore_wait(barrier, len(moves))
        copies = []
        for order, ((dz, db), target) in enumerate(zip(moves, targets)):
            copy = pltpu.make_async_remote_copy(
                src_ref=x_ref if pick is None else x_ref.at[pick(*target)],
                dst_ref=o_ref.at[slot(dz, db, zone, band)],
                send_sem=send_sem.at[order],
                recv_sem=recv_sem.at[order],
                device_id=target,
                device_id_type=pl.DeviceIdType.MESH,
            )
            copy.start()
            copies.append(copy)
        own.wait()
        for copy in copies:
            copy.wait()
        if label_row is not None:
            code_ref = refs[0]
            groups = piece[0] // ROWS
            for order in range(slots * groups):
                at = order % groups * ROWS + label_row
                code_ref[order : order + 1, :] = o_ref[order // groups, at : at + 1, :].astype(
                    jnp.int32
                )

    out_shape = [jax.ShapeDtypeStruct((slots,) + piece, block.dtype)]
    if label_row is not None:
        out_shape.append(jax.ShapeDtypeStruct((slots * piece[0] // ROWS, LANES), jnp.int32))
    return pl.pallas_call(
        kernel,
        out_shape=out_shape,
        in_specs=[VMEM],
        out_specs=[VMEM] * len(out_shape),
        scratch_shapes=[
            pltpu.SemaphoreType.DMA((len(moves),)),
            pltpu.SemaphoreType.DMA((len(moves),)),
            pltpu.SemaphoreType.DMA,
        ],
        compiler_params=pltpu.CompilerParams(collective_id=ident, has_side_effects=True),
    )(block)


def lane_take(row, index):
    table = jnp.broadcast_to(row, index.shape)
    return jnp.take_along_axis(table, index, axis=1, mode="promise_in_bounds")


def lookup(rows, index):
    found = jnp.zeros(index.shape, rows[0].dtype)
    low = index & (LANES - 1)
    for part, row in enumerate(rows):
        found = jnp.where(index // LANES == part, lane_take(row, low), found)
    return found


class Catalog:
    def __init__(self, sources, edge, blobs):
        self.parts = sources // LANES
        self.edge_row = 2 * self.parts
        self.count_row = self.edge_row + 1
        self.member_row = -(-(self.count_row + 1) // 8) * 8
        self.member_rows = blobs // PACK
        self.rows = self.member_row + -(-self.member_rows // 8) * 8
        self.sources, self.edge, self.blobs = sources, edge, blobs

    def pack(self, source_ref, edge_ref, member_ref, count_ref, sigma_ref, out_ref, spread_ref):
        out_ref[...] = jnp.zeros_like(out_ref)
        for coord in range(2):
            for part in range(self.parts):
                at = coord * self.parts + part
                out_ref[at : at + 1, :] = source_ref[
                    coord : coord + 1, part * LANES : (part + 1) * LANES
                ]
        out_ref[self.edge_row : self.edge_row + 1, :] = edge_ref[...].astype(jnp.float32)
        out_ref[self.count_row : self.count_row + 1, : self.blobs] = count_ref[...].astype(
            jnp.float32
        )
        seats = [
            member_ref[pl.ds(seat, self.member_rows, stride=PACK), :].astype(jnp.float32)
            for seat in range(PACK)
        ]
        out_ref[self.member_row : self.member_row + self.member_rows, :] = jnp.concatenate(
            seats, axis=1
        )
        sigma = sigma_ref[...]
        spread_ref[...] = 0.5 / (sigma * sigma)

    def members(self, ref, zone):
        return ref[zone, self.member_row : self.member_row + self.member_rows, :].astype(jnp.int32)

    def edges(self, ref, zone):
        return ref[zone, self.edge_row : self.edge_row + 1, :].astype(jnp.int32)

    def live(self, ref, zone):
        shape = (self.member_rows, LANES)
        lane = lax.broadcasted_iota(jnp.int32, shape, 1)
        row = lax.broadcasted_iota(jnp.int32, shape, 0)
        counts = ref[zone, self.count_row : self.count_row + 1, :].astype(jnp.int32)
        held = lane_take(counts, row * PACK + lane // MAX_SOURCES)
        return (lane % MAX_SOURCES) < held


def resolve(cat, zones, cat_ref, edge_ref, table_ref):
    def edge_body(zone, carry):
        index = jnp.broadcast_to(cat.edges(cat_ref, zone), (8, LANES))
        for coord in range(2):
            rows = [
                cat_ref[zone, coord * cat.parts + part : coord * cat.parts + part + 1, :]
                for part in range(cat.parts)
            ]
            edge_ref[coord, zone] = lookup(rows, index)
        return carry

    lax.fori_loop(0, zones, edge_body, 0)

    def member_body(zone, carry):
        member = cat.members(cat_ref, zone)
        before = jnp.maximum(zone - 1, 0)
        after = jnp.minimum(zone + 1, zones - 1)
        lane = lax.broadcasted_iota(jnp.int32, (8, LANES), 1)
        low = member < cat.edge
        high = member >= cat.edge + cat.sources
        own = jnp.clip(member - cat.edge, 0, cat.sources - 1)
        rim = jnp.where(low, cat.edge + member, jnp.where(high, member - cat.edge - cat.sources, 0))
        start = pl.multiple_of(zone * cat.member_rows, 8)
        for coord in range(2):
            rows = [
                cat_ref[zone, coord * cat.parts + part : coord * cat.parts + part + 1, :]
                for part in range(cat.parts)
            ]
            table = jnp.where(lane >= cat.edge, edge_ref[coord, before], edge_ref[coord, after])
            at_rim = lane_take(table[:1], rim)
            table_ref[coord, pl.ds(start, cat.member_rows), :] = jnp.where(
                low | high, at_rim, lookup(rows, own)
            )
        table_ref[2, pl.ds(start, cat.member_rows), :] = cat.live(cat_ref, zone).astype(jnp.float32)
        return carry

    lax.fori_loop(0, zones, member_body, 0)


def tile_kernel(
    cat, zones, groups,
    blob_ref, band_ref, shift_ref, amp_ref, spread_ref,
    cat_ref, pixel_ref, weight_ref,
    out_ref, edge_ref, table_ref, line_ref, used_ref,
):
    step = pl.program_id(0)
    height = pixel_ref.shape[1]

    @pl.when(step == 0)
    def _():
        out_ref[...] = jnp.zeros_like(out_ref)
        for zone in range(zones):
            used_ref[zone] = 0
        resolve(cat, zones, cat_ref, edge_ref, table_ref)

    half = MAX_SOURCES // 2
    shape = (MAX_SOURCES, LANES)
    lane = lax.broadcasted_iota(jnp.int32, shape, 1)
    sub = lax.broadcasted_iota(jnp.int32, shape, 0)
    lane_f = lane.astype(jnp.float32)
    keep = (lane % half) == (sub % half)
    tall = (height, LANES)
    tall_lane = lax.broadcasted_iota(jnp.int32, tall, 1)
    row_f = lax.broadcasted_iota(jnp.int32, tall, 0).astype(jnp.float32)
    eight_lane = tall_lane[:8]
    comp = (eight_lane[:1] // half) % COMPS
    width = COMPS * half
    high_part = (tall_lane < width) | (tall_lane >= 2 * width)
    used_part = tall_lane < 3 * width
    blank = jnp.zeros((LANES - 3 * width, LANES), jnp.float32)

    for slot in range(pixel_ref.shape[0]):
        tile = step * pixel_ref.shape[0] + slot
        blob = blob_ref[tile]
        at = blob // PACK
        offset = (blob % PACK) * MAX_SOURCES
        table = [
            jnp.broadcast_to(table_ref[k, pl.ds(at, 1), :], shape) for k in range(3)
        ]
        col_pos = jnp.sum(
            jnp.where(lane == offset + sub, table[1], 0.0), axis=1, keepdims=True
        )
        spread = [spread_ref[g, tile] for g in range(COMPS)]
        amp = [amp_ref[g, tile] for g in range(COMPS)]
        row_spread = jnp.where(comp == 0, spread[0], jnp.where(comp == 1, spread[1], spread[2]))
        row_amp = jnp.where(comp == 0, amp[0], jnp.where(comp == 1, amp[1], amp[2]))
        dcol = lane_f - shift_ref[1, tile] - col_pos
        dcol = dcol * dcol
        cols = [jnp.exp(-spread[g] * dcol) for g in range(COMPS)]
        cols_head = [col.astype(jnp.bfloat16).astype(jnp.float32) for col in cols]
        cols_tail = [col - head for col, head in zip(cols, cols_head)]
        root = jnp.sqrt(weight_ref[slot])
        image = root * pixel_ref[slot]
        image_head = image.astype(jnp.bfloat16).astype(jnp.float32)
        line_ref[slot, 0] = root
        line_ref[slot, 1] = image_head
        line_ref[slot, 2] = image - image_head
        rights = []
        for h in range(2):
            index = offset + h * half + eight_lane % half
            row_pos = jnp.take_along_axis(table[0][:8], index, axis=1, mode="promise_in_bounds")
            live = jnp.take_along_axis(table[2][:8], index, axis=1, mode="promise_in_bounds")
            drow = row_f - shift_ref[0, tile] - row_pos[:1]
            rows = jnp.exp(-row_spread * (drow * drow)) * (row_amp * live[:1])
            rows_head = rows.astype(jnp.bfloat16).astype(jnp.float32)
            line_ref[slot, 3 + h] = jnp.where(
                used_part, jnp.where(high_part, rows_head, rows - rows_head), 0.0
            )
            span = slice(h * half, (h + 1) * half)
            heads = [c[span] for c in cols_head]
            rights.append(
                jnp.concatenate(
                    heads + heads + [c[span] for c in cols_tail] + [blank], axis=0
                ).astype(jnp.bfloat16)
            )

        def render(chunk):
            models = []
            for h in range(2):
                left = []
                for i in range(chunk * CHUNK, (chunk + 1) * CHUNK, 2):
                    pair = jnp.concatenate(
                        [
                            jnp.broadcast_to(
                                line_ref[slot, 3 + h, i + d : i + d + 1, :], (half, LANES)
                            )
                            for d in range(2)
                        ],
                        axis=0,
                    )
                    left.append(jnp.where(keep, pair, 0.0).astype(jnp.bfloat16))
                models.append(
                    lax.dot_general(
                        jnp.concatenate(left, axis=0), rights[h], (((1,), (0,)), ((), ())),
                        preferred_element_type=jnp.float32,
                    )
                )
            return models

        product = None
        chunks = height // CHUNK
        ahead = render(0)
        for chunk in range(chunks):
            models = ahead
            if chunk + 1 < chunks:
                ahead = render(chunk + 1)
            heads, tails, lines = [], [], []
            for at_row in range(CHUNK):
                i = chunk * CHUNK + at_row
                span = slice(at_row * half, (at_row + 1) * half)
                weight = jnp.broadcast_to(line_ref[slot, 0, i : i + 1, :], shape)
                scaled = jnp.concatenate([models[0][span], models[1][span]], axis=0) * weight
                head = scaled.astype(jnp.bfloat16)
                heads.append(head)
                tails.append((scaled - head.astype(jnp.float32)).astype(jnp.bfloat16))
                lines.append(
                    jnp.concatenate(
                        [
                            jnp.broadcast_to(line_ref[slot, k, i : i + 1, :], (half, LANES))
                            for k in (1, 2)
                        ],
                        axis=0,
                    ).astype(jnp.bfloat16)
                )
            factor = jnp.concatenate(
                [jnp.concatenate(heads, axis=1), jnp.concatenate(tails, axis=1)], axis=0
            )
            left = jnp.concatenate([factor, jnp.concatenate(lines, axis=1)], axis=0)
            part = lax.dot_general(
                left, factor, (((1,), (1,)), ((), ())), preferred_element_type=jnp.float32
            )
            product = part if product is None else product + part
        folded = product[:, :16] + product[:, 16:]
        normal = folded[:16] + folded[16:32]
        vector = folded[32:40] + folded[40:48]
        zone = blob // cat.blobs
        code = band_ref[tile] * cat.blobs + blob % cat.blobs
        eight = lax.broadcasted_iota(jnp.int32, vector.shape, 0)
        tailrows = jnp.where(
            eight == 0, vector, jnp.where(eight == 1, code.astype(jnp.float32), 0.0)
        )
        entry = jnp.concatenate([normal, tailrows], axis=0)
        entry = jnp.concatenate(
            [entry, jnp.zeros((ROWS, LANES - MAX_SOURCES), jnp.float32)], axis=1
        )
        order = used_ref[zone]
        used_ref[zone] = order + 1
        seat = order % PACK
        entry = pltpu.roll(entry, seat * MAX_SOURCES, 1)
        place = zone * groups + order // PACK
        out_ref[place] = out_ref[place] + entry


def tile_terms(cat, zones, groups, blob, band, shift, amp, spread, catalogs, pixels, weights):
    tiles, height, width = pixels.shape
    per = TILES_STEP
    while tiles % per:
        per -= 1
    block = pl.BlockSpec((per, height, width), lambda s: (s, 0, 0))
    return pl.pallas_call(
        functools.partial(tile_kernel, cat, zones, groups),
        grid=(tiles // per,),
        out_shape=jax.ShapeDtypeStruct((zones * groups, ROWS, LANES), jnp.float32),
        in_specs=[SMEM] * 5 + [VMEM, block, block],
        out_specs=pl.BlockSpec((zones * groups, ROWS, LANES), lambda s: (0, 0, 0)),
        scratch_shapes=[
            pltpu.VMEM((2, zones, 8, LANES), jnp.float32),
            pltpu.VMEM((3, zones * cat.member_rows, LANES), jnp.float32),
            pltpu.VMEM((per, 5, height, width), jnp.float32),
            pltpu.SMEM((zones,), jnp.int32),
        ],
        compiler_params=pltpu.CompilerParams(dimension_semantics=("arbitrary",)),
    )(blob, band, shift, amp, spread, catalogs, pixels, weights)


def gather_kernel(capacity, groups, code_ref, got_ref, total_ref):
    total_ref[...] = jnp.zeros_like(total_ref)
    lane = lax.broadcasted_iota(jnp.int32, (ROWS, LANES), 1) // MAX_SOURCES

    def body(group, carry):
        block = got_ref[group]
        for seat in range(min(PACK, capacity)):
            code = code_ref[group, seat * MAX_SOURCES]
            to = code % PACK
            moved = pltpu.roll(block, ((to - seat + PACK) % PACK) * MAX_SOURCES, 1)
            place = code // PACK
            total_ref[place] = total_ref[place] + jnp.where(lane == to, moved, 0.0)
        return carry

    lax.fori_loop(0, got_ref.shape[0], body, 0)


def solve_group(block):
    row = lax.broadcasted_iota(jnp.int32, (ROWS, LANES), 0)
    lane = lax.broadcasted_iota(jnp.int32, (ROWS, LANES), 1)
    column = lane % MAX_SOURCES
    first = lane - column
    block = block + jnp.where(row == column, PRIOR, 0.0)
    scale = jnp.ones((1, LANES), jnp.float32)
    for k in range(MAX_SOURCES):
        taken = jnp.take_along_axis(block, first + k, axis=1, mode="promise_in_bounds")
        pivot = taken[k : k + 1]
        across = block[k : k + 1]
        scale = jnp.where(column[:1] == k, across, scale)
        ratio = jnp.where(column[:1] == k, 0.0, across / pivot)
        block = block - taken * ratio
    return block[MAX_SOURCES : MAX_SOURCES + 1] / scale


def finish_kernel(
    cat, zones, bands, share, total_ref, cat_ref, out_ref,
    got_ref, solved_ref, flux_ref, pick_ref,
    send_sum, recv_sum, own_sum, send_flux, recv_flux, own_flux,
):
    zone = lax.axis_index("zone")
    band = lax.axis_index("band")
    moves = [(dz, db) for dz in (0, 1, -1) for db in range(bands) if dz or db]
    targets = [
        (lax.rem(zone + dz + zones, zones), lax.rem(band + db, bands)) for dz, db in moves
    ]
    barrier = pltpu.get_barrier_semaphore()
    for target in targets:
        pl.semaphore_signal(barrier, inc=1, device_id=target, device_id_type=pl.DeviceIdType.MESH)
    own = pltpu.make_async_copy(total_ref.at[band], got_ref.at[band], own_sum)
    own.start()
    pl.semaphore_wait(barrier, len(moves))
    sums = []
    for order in range(bands - 1):
        target = targets[order]
        copy = pltpu.make_async_remote_copy(
            src_ref=total_ref.at[target[1]],
            dst_ref=got_ref.at[band],
            send_sem=send_sum.at[order],
            recv_sem=recv_sum.at[order],
            device_id=target,
            device_id_type=pl.DeviceIdType.MESH,
        )
        copy.start()
        sums.append(copy)

    edges = cat.edges(cat_ref, zone)
    rows = cat.member_rows
    source = lax.broadcasted_iota(jnp.int32, (cat.sources, LANES), 0)
    for side in range(3):
        near = lax.rem(zone + side - 1 + zones, zones)
        member = cat.members(cat_ref, near)
        live = cat.live(cat_ref, near)
        if side == 0:
            valid = (member >= cat.edge + cat.sources) & (zone > 0)
            target = lane_take(edges, jnp.where(valid, member - cat.edge - cat.sources, 0))
        elif side == 1:
            valid = (member >= cat.edge) & (member < cat.edge + cat.sources)
            target = member - cat.edge
        else:
            valid = (member < cat.edge) & (zone < zones - 1)
            target = lane_take(edges, jnp.where(valid, member + cat.edge, 0))
        target = jnp.where(valid & live, target, -1)
        for row in range(rows):
            hit = source == target[row : row + 1, :]
            pick_ref[side, :, row * LANES : (row + 1) * LANES] = jnp.where(hit, 1.0, 0.0).astype(
                jnp.bfloat16
            )

    own.wait()
    for copy in sums:
        copy.wait()
    for group in range(share):
        span = slice(group * ROWS, (group + 1) * ROWS)
        block = got_ref[0, span, :]
        for other in range(1, bands):
            block = block + got_ref[other, span, :]
        solved_ref[group : group + 1, :] = solve_group(block)
    if solved_ref.shape[0] > share:
        solved_ref[share:, :] = jnp.zeros((solved_ref.shape[0] - share, LANES), jnp.float32)

    own = pltpu.make_async_copy(solved_ref, flux_ref.at[bands + band], own_flux)
    own.start()
    copies = []
    for order, ((dz, db), target) in enumerate(zip(moves, targets)):
        copy = pltpu.make_async_remote_copy(
            src_ref=solved_ref,
            dst_ref=flux_ref.at[(1 - dz) * bands + band],
            send_sem=send_flux.at[order],
            recv_sem=recv_flux.at[order],
            device_id=target,
            device_id_type=pl.DeviceIdType.MESH,
        )
        copy.start()
        copies.append(copy)
    own.wait()
    for copy in copies:
        copy.wait()

    total = jnp.zeros((16, cat.sources), jnp.float32)
    for side in range(3):
        parts = []
        for band_row in range(FILTER_BANDS):
            lines = []
            for row in range(rows):
                group = band_row * rows + row
                at = group % share
                lines.append(flux_ref[side * bands + group // share, at : at + 1, :])
            parts.append(jnp.concatenate(lines, axis=1))
        values = jnp.concatenate(parts, axis=0)
        pieces = []
        for _ in range(3):
            piece = values.astype(jnp.bfloat16).astype(jnp.float32)
            values = values - piece
            pieces.append(piece)
        pieces.append(jnp.zeros((16 - 3 * FILTER_BANDS, values.shape[1]), jnp.float32))
        left = jnp.concatenate(pieces, axis=0).astype(jnp.bfloat16)
        total = total + lax.dot_general(
            left, pick_ref[side], (((1,), (1,)), ((), ())), preferred_element_type=jnp.float32
        )
    out_ref[...] = total[0:3] + total[3:6] + total[6:9]


def on_device(
    sizes, pixels, inv_var, tile_offset, psf_amp, psf_sigma, tile_blob, tile_band,
    source_pos, edge_rows, blob_members, sources_per_blob,
):
    zones, bands = sizes
    blobs = sources_per_blob.shape[0]
    sources = source_pos.shape[1]
    tiles = pixels.shape[0]
    cat = Catalog(sources, edge_rows.shape[0] // 2, blobs)
    capacity = max(2, (2 * tiles + zones - 1) // zones)
    groups = -(-capacity // PACK)
    systems = FILTER_BANDS * blobs // PACK
    share = systems // bands
    zone_moves = [(d, 0) for d in range(1, zones)]

    packed, spread = pl.pallas_call(
        cat.pack,
        out_shape=(
            jax.ShapeDtypeStruct((cat.rows, LANES), jnp.float32),
            jax.ShapeDtypeStruct(psf_sigma.shape, jnp.float32),
        ),
        in_specs=[VMEM] * 5,
        out_specs=(VMEM, VMEM),
    )(
        source_pos, edge_rows.reshape(1, -1), blob_members, sources_per_blob.reshape(1, -1),
        psf_sigma,
    )
    (catalogs,) = exchange(packed, zone_moves, None, lambda dz, db, z, b: z, zones, sizes, 0)
    terms = tile_terms(
        cat, zones, groups, tile_blob, tile_band, tile_offset, psf_amp, spread, catalogs,
        pixels, inv_var,
    )
    got, codes = exchange(
        terms.reshape(zones, groups * ROWS, LANES),
        zone_moves, lambda z, b: z, lambda dz, db, z, b: z, zones, sizes, 1,
        MAX_SOURCES + 1,
    )
    got = got.reshape(zones * groups, ROWS, LANES)
    totals = pl.pallas_call(
        functools.partial(gather_kernel, capacity, groups),
        out_shape=jax.ShapeDtypeStruct((systems, ROWS, LANES), jnp.float32),
        in_specs=[SMEM, VMEM],
        out_specs=VMEM,
    )(codes, got)
    near = 3 * bands - 1
    seats = -(-share // 8) * 8
    return pl.pallas_call(
        functools.partial(finish_kernel, cat, zones, bands, share),
        out_shape=jax.ShapeDtypeStruct((FILTER_BANDS, sources), jnp.float32),
        in_specs=[VMEM, VMEM],
        out_specs=VMEM,
        scratch_shapes=[
            pltpu.VMEM((bands, share * ROWS, LANES), jnp.float32),
            pltpu.VMEM((seats, LANES), jnp.float32),
            pltpu.VMEM((3 * bands, seats, LANES), jnp.float32),
            pltpu.VMEM((3, sources, cat.member_rows * LANES), jnp.bfloat16),
            pltpu.SemaphoreType.DMA((bands - 1,)),
            pltpu.SemaphoreType.DMA((bands - 1,)),
            pltpu.SemaphoreType.DMA,
            pltpu.SemaphoreType.DMA((near,)),
            pltpu.SemaphoreType.DMA((near,)),
            pltpu.SemaphoreType.DMA,
        ],
        compiler_params=pltpu.CompilerParams(collective_id=2, has_side_effects=True),
    )(totals.reshape(bands, share * ROWS, LANES), catalogs)


def solution(mesh):
    sizes = (mesh.shape["zone"], mesh.shape["band"])
    return jax.shard_map(
        functools.partial(on_device, sizes),
        mesh=mesh,
        in_specs=(
            P(("zone", "band"), None, None),
            P(("zone", "band"), None, None),
            P(None, ("zone", "band")),
            P(None, ("zone", "band")),
            P(None, ("zone", "band")),
            P(("zone", "band")),
            P(("zone", "band")),
            P(None, "zone"),
            P("zone"),
            P("zone", None),
            P("zone"),
        ),
        out_specs=P(None, "zone"),
        check_vma=False,
    )
```
